128 devices in a mesh: seg: 4 (over x_hi, core), chan: 32 (over z, y, x_lo).
Axes of the slice: x: 4 (x_hi: 2, x_lo: 2; x = x_hi * 2 + x_lo), y: 4, z: 4, core: 2. Of those that a mesh axis runs over, the one named last changes fastest.
Arguments:
- traces: bfloat16 [32, 4096, 4096], P('seg', 'chan'), may hold values from -6 to 6
- channel_mask: int32 [4096], P('chan'), may hold values 0 or 1
- owner_ids: int32 [32, 64, 1], P('chan'), may hold values from 0 to 31; in each aligned block of 64 rows (0 to 63, 64 to 127, ..., all dimensions but the last counted through in order) at most 4 rows name the same one
- local_bins: int32 [32, 64], P('chan'), may hold values from 0 to 7
Outputs:
- stacks: float32 [256, 2048], P('chan')
The draws below stay inside these ranges and needn't reach their ends.
Inputs may be any that keep to these rules, and one draw needn't show every extreme that they name: `owner_ids`: among the 64 tiles of one block no owner is named more than 4 times, a bound that some block reaches.
All inputs are finite; a program needn't handle non-finite values. No bound on the sum of `channel_mask` on one device may be relied on, other than what follows from the above.
Results may differ from the reference program's by a relative error of at most 0.0053.
Values may be sent and summed in bfloat16 or wider, within the bound.
A program may use at most 192 MiB of HBM per device.

```python
import math
import jax
import jax.numpy as jnp
import numpy as np
from jax import lax

CB = 128
NT = 4096
DEC = 2
K0 = 8
HW = 64
R = 4
G = 16
BIN_DEV = 8
NB = 1024
NLAG = 2048
TILES = 64
SEGS = 32
NBLK = 32
CHANNELS = 4096
NBIN = 256
CAP = 4
N_CHAN = 32


def with_ends(values, rng, least, high):
    index_at = [jax.random.randint(jax.random.fold_in(rng, axis), (), 0, length) for axis, length in enumerate(values.shape)]
    main_axis = values.shape.index(max(values.shape))
    neighbour = index_at[:main_axis] + [(index_at[main_axis] + 1) % values.shape[main_axis]] + index_at[main_axis + 1:]
    return values.at[tuple(index_at)].set(least).at[tuple(neighbour)].set(high)


def level_of(own_key, dims, split, low, high):
    loudness, own = 1.0, jax.random.fold_in(own_key, 6)
    for dim, shards_of in split:
        steps = jnp.exp(jax.random.uniform(jax.random.fold_in(own, dim), (shards_of,), jnp.float32, low / len(split), high / len(split)))
        loudness = loudness * jnp.repeat(steps, dims[dim] // shards_of).reshape([-1 if axis == dim else 1 for axis in range(len(dims))])
    return loudness


def deal_out(rng, own, number, rows, count, top, most, slope):
    ranking = jax.random.permutation(rng, count)
    heavy_load, usual = portions_of(count, rows * top, most, slope, True), portions_of(count, rows * top, most, slope, False)
    places = jnp.arange(count)

    def named(lengths, offset_by):
        used = int((lengths > 0).sum())
        fixed = max(1, used // 4)
        shifted = fixed + (places - fixed + offset_by * (used - fixed)) % max(1, count - fixed)
        return jnp.zeros((count,), jnp.int32).at[ranking[jnp.where(places < fixed, places, shifted)]].set(jnp.asarray(lengths, jnp.int32))

    lengths = jnp.where(number % 4 == 0, named(heavy_load, number // 4), named(usual, number - number // 4 - 1))
    mixed = jax.random.permutation(jax.random.fold_in(own, 3), count)
    source_of, receiver = mixed[0:count // 2 * 2:2], mixed[1:count // 2 * 2:2]
    slack = jnp.minimum(lengths[source_of] - 1, most - lengths[receiver]) // 2
    slack = jnp.where((source_of == ranking[0]) | (receiver == ranking[0]) | (lengths[receiver] == 0), 0, jnp.maximum(slack, 0))
    shifted = jax.random.randint(jax.random.fold_in(own, 4), (count // 2,), 0, 1 << 20) % (slack + 1)
    lengths = lengths.at[source_of].add(-shifted).at[receiver].add(shifted)
    items = jnp.searchsorted(jnp.cumsum(lengths), jnp.arange(rows * top), side="right").astype(jnp.int32)
    table = items.reshape(top, rows).T
    table = table[jax.random.permutation(jax.random.fold_in(own, 1), rows)]
    offset_by = jax.random.randint(jax.random.fold_in(own, 2), (rows, 1), 0, top)
    return jnp.take_along_axis(table, (jnp.arange(top)[None, :] + offset_by) % top, axis=1)


def portions_of(count, total, reach, lean, full):
    weights = [(1 << 20) // math.isqrt(rank ** lean) + 1 for rank in range(1, count + 1)]
    largest = reach if full else min(reach, max(-(-total // count), total * weights[0] // sum(weights)))
    least = 1 if total - largest >= count - 1 else 0
    given, spare = [largest] + [least] * (count - 1), total - largest - least * (count - 1)
    while spare > 0:
        movable = [i for i in range(1, count) if given[i] < largest] or [i for i in range(1, count) if given[i] < reach]
        whole, budget = sum([weights[i] for i in movable]), spare
        for i in movable:
            extra = min(reach - given[i], max(1, budget * weights[i] // whole), spare)
            given[i] = given[i] + extra
            spare = spare - extra
    return np.array(given)


def noise(rng, dims, spread, reach, cuts=(), held_as=jnp.bfloat16):
    gain = level_of(rng, dims, cuts, -0.22, 0.18) if cuts else 1.0
    values = jax.random.normal(rng, dims, jnp.float32) * spread * gain
    return jnp.minimum(jnp.maximum(values, -reach), reach).astype(held_as)


def setup_inputs(seed: int = 0) -> dict:
    arg_keys = jax.random.split(jax.random.key(seed), 5)
    traces = noise(arg_keys[0], (SEGS, CHANNELS, NT), 1.0, 6.0, ((0, 4), (1, 32)))
    channel_mask = with_ends((jax.random.randint(arg_keys[1], (CHANNELS,), 0, 4) < 3).astype(jnp.int32), jax.random.fold_in(arg_keys[1], 1), 0, 1)
    owner_ids_keys = jax.random.split(jax.random.fold_in(arg_keys[2], 1), NBLK * TILES // TILES)
    owner_ids_turns = jax.random.permutation(jax.random.fold_in(arg_keys[2], 3), NBLK * TILES // TILES)
    owner_ids = jax.vmap(lambda own, number: deal_out(jax.random.fold_in(arg_keys[2], 2), own, number, TILES, N_CHAN, 1, CAP, 2))(owner_ids_keys, owner_ids_turns).reshape((NBLK, TILES, 1))
    local_bins = with_ends(jax.random.randint(arg_keys[3], (NBLK, TILES), 0, BIN_DEV), jax.random.fold_in(arg_keys[3], 1), 0, BIN_DEV - 1).astype(jnp.int32)
    return {"traces": traces, "channel_mask": channel_mask, "owner_ids": owner_ids, "local_bins": local_bins}


EPSILON = 1e-06

def forward_table():
    samples = jnp.arange(NT, dtype=jnp.int32)
    freqs = K0 + jnp.arange(NB, dtype=jnp.int32)
    phase = samples[:, None] * freqs[None, :] % NT
    angle = phase.astype(jnp.float32) * (2.0 * math.pi / NT)
    return jnp.concatenate([jnp.cos(angle), -jnp.sin(angle)], axis=1).astype(jnp.bfloat16)

def band_table():
    freqs = jnp.arange(NB, dtype=jnp.int32)
    return (jnp.abs(freqs[:, None] - freqs[None, :]) <= HW).astype(jnp.float32)

def inverse_table():
    freqs = K0 + jnp.arange(NB, dtype=jnp.int32)
    delays = (jnp.arange(NLAG, dtype=jnp.int32) - NLAG // 2) * DEC
    phase = jnp.mod(freqs[:, None] * delays[None, :], NT)
    angle = phase.astype(jnp.float32) * (2.0 * math.pi / NT)
    scale = 1.0 / math.sqrt(NB)
    return jnp.concatenate([jnp.cos(angle) * scale, -jnp.sin(angle) * scale], axis=0)

def whiten(block, mask_float, table, band):
    segs, chans, length = block.shape
    spectrum = jnp.dot(block.reshape(segs * chans, length), table, preferred_element_type=jnp.float32)
    half = spectrum.shape[1] // 2
    real_part = spectrum[:, :half]
    imag_part = spectrum[:, half:]
    power = real_part * real_part + imag_part * imag_part
    counts = lax.optimization_barrier(jnp.sum(band, axis=0))
    level = jnp.sqrt(jnp.dot(power, band, precision=lax.Precision.HIGHEST) / counts + EPSILON)
    weight = jnp.tile(mask_float, segs)[:, None] / level
    result = jnp.concatenate([real_part * weight, imag_part * weight], axis=1)
    return result.astype(jnp.bfloat16).reshape(segs, chans, 2 * half)

def cross(source, source_mask, target, target_mask, total_segs):
    half = source.shape[-1] // 2
    source_float = source.astype(jnp.float32)
    target_float = target.astype(jnp.float32)
    source_real = source_float[..., :half]
    source_imag = source_float[..., half:]
    target_real = target_float[..., :half]
    target_imag = target_float[..., half:]
    real_sum = lax.optimization_barrier(jnp.sum(source_real * target_real + source_imag * target_imag, axis=0))
    imag_sum = lax.optimization_barrier(jnp.sum(source_imag * target_real - source_real * target_imag, axis=0))
    chans = real_sum.shape[0]
    real_groups = real_sum.reshape(G, chans // G, half).sum(axis=1)
    imag_groups = imag_sum.reshape(G, chans // G, half).sum(axis=1)
    counts = (source_mask * target_mask).reshape(G, chans // G).sum(axis=1)
    scale = 1.0 / (total_segs * jnp.maximum(counts, 1.0))
    return jnp.concatenate([real_groups, imag_groups], axis=1) * scale[:, None]

def reference(traces, channel_mask, owner_ids, local_bins):
    table = forward_table()
    band = band_table()
    masks = channel_mask.astype(jnp.float32).reshape(NBLK, CB)

    def whiten_block(index):
        block = lax.dynamic_slice_in_dim(traces, index * CB, CB, 1)
        row_mask = lax.dynamic_index_in_dim(masks, index, 0, keepdims=False)
        return whiten(block, row_mask, table, band)
    whitened = lax.map(whiten_block, jnp.arange(NBLK, dtype=jnp.int32))
    padded = jnp.concatenate([whitened, jnp.zeros((R,) + whitened.shape[1:], jnp.bfloat16)], axis=0)
    padded_masks = jnp.concatenate([masks, jnp.zeros((R, CB), jnp.float32)], axis=0)

    def block_tiles(index):
        source = lax.dynamic_index_in_dim(padded, index, 0, keepdims=False)
        source_mask = lax.dynamic_index_in_dim(padded_masks, index, 0, keepdims=False)
        pieces = []
        for offset in range(1, R + 1):
            target = lax.dynamic_index_in_dim(padded, index + offset, 0, keepdims=False)
            target_mask = lax.dynamic_index_in_dim(padded_masks, index + offset, 0, keepdims=False)
            pieces.append(cross(source, source_mask, target, target_mask, SEGS))
        return jnp.concatenate(pieces, axis=0)
    tiles = lax.map(block_tiles, jnp.arange(NBLK, dtype=jnp.int32))
    lags = jnp.dot(tiles.reshape(NBLK * TILES, 2 * NB), inverse_table(), precision=lax.Precision.HIGHEST)
    labels = (owner_ids.reshape(-1) * BIN_DEV + local_bins.reshape(-1)).astype(jnp.int32)
    return jax.ops.segment_sum(lags, labels, num_segments=NBIN)
```

```python
import functools
import math

import jax
import jax.numpy as jnp
import numpy as np
from jax import lax
from jax.experimental import pallas as pl
from jax.experimental.pallas import tpu as pltpu
from jax.sharding import PartitionSpec as P

CB = 128
NT = 4096
K0 = 8
HW = 64
R = 4
G = 16
BIN_DEV = 8
NB = 1024
NLAG = 2048
HALF = NB // 2
EPSILON = 1e-06
STEPS = 4
MESH = pl.DeviceIdType.MESH


def small_tables():
    freqs = K0 + np.arange(NB)
    coarse = (np.arange(16)[:, None, None] * 64 * freqs[None, None, :]) % NT * (2.0 * math.pi / NT)
    fine = (np.arange(64)[:, None] * freqs[None, :]) % NT * (2.0 * math.pi / NT)
    return [
        jnp.asarray(t, jnp.float32)
        for t in (np.cos(coarse), -np.sin(coarse), np.cos(fine), -np.sin(fine))
    ]


def peer(c, r):
    x, y, z = c % 2, (c // 2) % 4, c // 8
    return ((z + r % 4) % 4) * 8 + ((y + (r // 4) % 4) % 4) * 2 + (x + r // 16) % 2


def spectra_kernel(
    traces, coarse_re, coarse_im, fine_re, fine_im, mask_ref,
    out_ref,
    x_ref, tab, spec, power, inv_level, send, recv, acc,
    x_sem, own_sem, send_sem, recv_sem,
):
    chans = lax.axis_size("chan")
    me = lax.axis_index("chan")
    segs = 8 // STEPS
    rows = segs * CB

    def load(i):
        part = pl.ds(i * segs, segs)
        return pltpu.make_async_copy(traces.at[part], x_ref.at[part], x_sem.at[i])

    for i in range(STEPS):
        load(i).start()

    barrier = pltpu.get_barrier_semaphore()

    def greet(r, carry):
        pl.semaphore_signal(barrier, inc=1, device_id={"chan": peer(me, r)}, device_id_type=MESH)
        return carry

    lax.fori_loop(1, chans, greet, 0)

    turn = lax.broadcasted_iota(jnp.int32, (64, 128), 1) % 4
    c0 = jnp.where(turn == 0, 1.0, jnp.where(turn == 2, -1.0, 0.0)).astype(jnp.bfloat16)
    c1 = jnp.where(turn == 1, 1.0, jnp.where(turn == 3, -1.0, 0.0)).astype(jnp.bfloat16)
    flip = jnp.where(turn % 2 == 0, 1.0, -1.0).astype(jnp.bfloat16)

    def make_rows(a, carry):
        for chunk in range(NB // 128):
            cols = pl.ds(chunk * 128, 128)
            ar, ai = coarse_re[a, :, cols], coarse_im[a, :, cols]
            br, bi = fine_re[:, cols], fine_im[:, cols]
            re = (ar * br - ai * bi).astype(jnp.bfloat16)
            im = (ar * bi + ai * br).astype(jnp.bfloat16)
            re1, im1 = re * c0 + im * c1, im * c0 - re * c1
            base = (chunk // 4) * NB + (chunk % 4) * 128
            for quarter, (u, v) in enumerate(
                ((re, im), (re1, im1), (re * flip, im * flip), (re1 * flip, im1 * flip))
            ):
                at = pl.ds(pl.multiple_of(quarter * 1024 + a * 64, 64), 64)
                tab[at, pl.ds(base, 128)] = u
                tab[at, pl.ds(base + HALF, 128)] = v
        return carry

    lax.fori_loop(0, 16, make_rows, 0)

    power[:, pl.ds(0, 128)] = jnp.zeros((rows, 128), jnp.bfloat16)
    power[:, pl.ds(128 + NB, 128)] = jnp.zeros((rows, 128), jnp.bfloat16)
    recv[:, pl.ds(chans, R)] = jnp.zeros((STEPS, R, 8 * segs, NB), jnp.bfloat16)
    near = (
        lax.broadcasted_iota(jnp.int32, (512, 256), 0)
        - lax.broadcasted_iota(jnp.int32, (512, 256), 1)
        - 128
    )
    band = jnp.where(jnp.abs(near) <= HW, 1.0, 0.0).astype(jnp.bfloat16)
    pl.semaphore_wait(barrier, chans - 1)

    def exchange(i, r):
        to = peer(me, r)
        return pltpu.make_async_remote_copy(
            send.at[i, to // 2, to % 2],
            recv.at[i, me],
            send_sem.at[i, to],
            recv_sem.at[i, me],
            device_id={"chan": to},
            device_id_type=MESH,
        )

    def arrival(i, r):
        source = peer(me, r)
        return pltpu.make_async_copy(recv.at[i, source], recv.at[i, source], recv_sem.at[i, source])

    def keep(i):
        return pltpu.make_async_copy(send.at[i, me // 2, me % 2], recv.at[i, me], own_sem.at[i])

    def whiten_step(i, carry):
        load(i).wait()

        def transform(n, carry):
            cols = pl.ds(pl.multiple_of(n * 256, 256), 256)
            block = x_ref[pl.ds(i * segs, segs)].reshape(rows, NT)
            spec[:, cols] = jnp.dot(block, tab[:, cols], preferred_element_type=jnp.float32)
            return carry

        lax.fori_loop(0, 2 * NB // 256, transform, 0)

        def add_power(n, carry):
            at = pl.ds(pl.multiple_of(n * 32, 32), 32)
            for chunk in range(NB // 256):
                base = (chunk // 2) * NB + (chunk % 2) * 256
                re, im = spec[at, pl.ds(base, 256)], spec[at, pl.ds(base + HALF, 256)]
                power[at, pl.ds(128 + chunk * 256, 256)] = (re * re + im * im).astype(jnp.bfloat16)
            return carry

        lax.fori_loop(0, rows // 32, add_power, 0)

        for chunk in range(NB // 256):
            total = jnp.dot(
                power[:, pl.ds(chunk * 256, 512)], band, preferred_element_type=jnp.float32
            )
            k = chunk * 256 + lax.broadcasted_iota(jnp.int32, (1, 256), 1)
            count = jnp.minimum(k + HW, NB - 1) - jnp.maximum(k - HW, 0) + 1
            inv_level[:, pl.ds(chunk * 256, 256)] = lax.rsqrt(
                total * (1.0 / count.astype(jnp.float32)) + EPSILON
            )

        def scale(g, carry):
            valid = mask_ref[pl.ds(pl.multiple_of(g * 8, 8), 8), :]
            for chunk in range(NB // 128):
                h, at = chunk // 4, (chunk % 4) * 128
                res, ims = [], []
                for s in range(segs):
                    row = pl.ds(pl.multiple_of(s * CB + g * 8, 8), 8)
                    weight = inv_level[row, pl.ds(chunk * 128, 128)] * valid
                    res.append(spec[row, pl.ds(h * NB + at, 128)] * weight)
                    ims.append(spec[row, pl.ds(h * NB + HALF + at, 128)] * weight)
                send[i, g, h, :, pl.ds(at, 128)] = jnp.concatenate(res, 0).astype(jnp.bfloat16)
                send[i, g, h, :, pl.ds(HALF + at, 128)] = jnp.concatenate(ims, 0).astype(jnp.bfloat16)
            return carry

        lax.fori_loop(0, G, scale, 0)

        def start(r, carry):
            exchange(i, r).start()
            return carry

        keep(i).start()
        lax.fori_loop(1, chans, start, 0)
        return carry

    lax.fori_loop(0, STEPS, whiten_step, 0)

    acc[...] = jnp.zeros_like(acc)

    def cross_step(i, carry):
        def take(r, carry):
            arrival(i, r).wait()
            return carry

        lax.fori_loop(1, chans, take, 0)
        keep(i).wait()

        def products(n, carry):
            chunk = n % 4
            first = (n // 4) * 4
            re_at = pl.ds(pl.multiple_of(chunk * 128, 128), 128)
            im_at = pl.ds(pl.multiple_of(HALF + chunk * 128, 128), 128)
            re = [recv[i, first + j, :, re_at].astype(jnp.float32) for j in range(4 + R)]
            im = [recv[i, first + j, :, im_at].astype(jnp.float32) for j in range(4 + R)]
            for j in range(4):
                for d in range(1, R + 1):
                    p = re[j] * re[j + d] + im[j] * im[j + d]
                    q = im[j] * re[j + d] - re[j] * im[j + d]
                    t = (first + j) * R + d - 1
                    acc[chunk, t, :, pl.ds(0, 128)] += p.reshape(segs, 8, 128).sum(0)
                    acc[chunk, t, :, pl.ds(128, 128)] += q.reshape(segs, 8, 128).sum(0)
            return carry

        lax.fori_loop(0, chans, products, 0)
        return carry

    lax.fori_loop(0, STEPS, cross_step, 0)

    def reduce_rows(n, carry):
        at = pl.ds(pl.multiple_of((n // 4) * 8, 8), 8)
        out_ref[n % 4, at, :] = acc[n % 4, at].sum(1)
        return carry

    lax.fori_loop(0, 4 * chans * R // 8, reduce_rows, 0)

    def finish(n, carry):
        exchange(n // chans, n % chans).wait_send()
        return carry

    for i in range(STEPS):
        lax.fori_loop(i * chans + 1, (i + 1) * chans, finish, 0)


def tile_sums(traces, mask_float):
    chans = lax.axis_size("chan")
    tiles = chans * R
    segs = traces.shape[0] // STEPS
    vmem = pl.BlockSpec(memory_space=pltpu.VMEM)
    return pl.pallas_call(
        spectra_kernel,
        out_shape=jax.ShapeDtypeStruct((4, tiles, 256), jnp.float32),
        in_specs=[pl.BlockSpec(memory_space=pl.ANY)] + [vmem] * 5,
        out_specs=vmem,
        scratch_shapes=[
            pltpu.VMEM(traces.shape, jnp.bfloat16),
            pltpu.VMEM((NT, 2 * NB), jnp.bfloat16),
            pltpu.VMEM((segs * CB, 2 * NB), jnp.float32),
            pltpu.VMEM((segs * CB, NB + 256), jnp.bfloat16),
            pltpu.VMEM((segs * CB, NB), jnp.float32),
            pltpu.VMEM((STEPS, G, 2, 8 * segs, NB), jnp.bfloat16),
            pltpu.VMEM((STEPS, chans + R, 8 * segs, NB), jnp.bfloat16),
            pltpu.VMEM((4, tiles, 8, 256), jnp.float32),
            pltpu.SemaphoreType.DMA((STEPS,)),
            pltpu.SemaphoreType.DMA((STEPS,)),
            pltpu.SemaphoreType.DMA((STEPS, chans)),
            pltpu.SemaphoreType.DMA((STEPS, chans)),
        ],
        compiler_params=pltpu.CompilerParams(
            collective_id=0, has_side_effects=True, vmem_limit_bytes=56 << 20
        ),
        name="spectra",
    )(traces, *small_tables(), jnp.broadcast_to(mask_float[:, None], (CB, 128)))


def inverse_rows(first_bin):
    freqs = K0 + first_bin + jnp.arange(128, dtype=jnp.int32)
    unit = 2.0 * math.pi / NT
    a = jnp.mod(freqs[:, None] * (jnp.arange(16, dtype=jnp.int32) * 128 - NLAG // 2)[None, :] * 2, NT)
    b = jnp.mod(freqs[:, None] * jnp.arange(128, dtype=jnp.int32)[None, :] * 2, NT)
    a, b = a.astype(jnp.float32) * unit, b.astype(jnp.float32) * unit
    scale = 1.0 / math.sqrt(NB)
    ca, sa = (jnp.cos(a) * scale)[:, :, None], (jnp.sin(a) * scale)[:, :, None]
    cb, sb = jnp.cos(b)[:, None, :], jnp.sin(b)[:, None, :]
    cos = (ca * cb - sa * sb).reshape(128, NLAG)
    sin = (sa * cb + ca * sb).reshape(128, NLAG)
    return jnp.concatenate([cos, -sin], axis=0)


def per_device(traces, channel_mask, owner_ids, local_bins):
    seg_count = lax.axis_size("seg")
    chan_count = lax.axis_size("chan")
    total_segs = traces.shape[0] * seg_count
    me = lax.axis_index("chan")
    group = me // 2
    labels = owner_ids.reshape(-1) * BIN_DEV + local_bins.reshape(-1)
    every = lax.all_gather(jnp.concatenate([channel_mask, labels]), "chan")
    masks = lax.dynamic_slice_in_dim(every[:, :CB].reshape(chan_count, G, 8), group, 1, 1)[:, 0]
    masks = jnp.pad(masks.astype(jnp.float32), ((0, R), (0, 0)))
    labels = lax.dynamic_slice_in_dim(every[:, CB:].reshape(chan_count, R, G), group, 1, 2)[..., 0]
    counts = jnp.stack(
        [(masks[:chan_count] * masks[d : d + chan_count]).sum(1) for d in range(1, R + 1)], 1
    )
    scale = 1.0 / (total_segs * jnp.maximum(counts, 1.0))
    bins = jnp.arange(chan_count * BIN_DEV, dtype=jnp.int32)
    stacker = jnp.where(bins[:, None] == labels.reshape(1, -1), scale.reshape(1, -1), 0.0)

    raw = tile_sums(traces, channel_mask.astype(jnp.float32))
    sums = lax.psum_scatter(raw, "seg", scatter_dimension=0, tiled=False)
    stacked = jnp.dot(stacker, sums, precision=lax.Precision.HIGHEST)
    arrived = lax.all_to_all(
        stacked.reshape(chan_count, BIN_DEV, 256), "chan", split_axis=0, concat_axis=0, tiled=True
    )
    spectra = arrived.reshape(G, 2, BIN_DEV, 256).sum(0)
    first = lax.axis_index("seg") * 128
    lags = jnp.dot(spectra[0], inverse_rows(first), precision=lax.Precision.HIGHEST)
    lags += jnp.dot(spectra[1], inverse_rows(first + HALF), precision=lax.Precision.HIGHEST)
    return lax.psum(lags, "seg")


def solution(mesh):
    in_specs = (P("seg", "chan", None), P("chan"), P("chan", None, None), P("chan", None))
    return jax.shard_map(
        per_device, mesh=mesh, in_specs=in_specs, out_specs=P("chan", None), check_vma=False
    )
```

```python
import functools
import math

import jax
import jax.numpy as jnp
import numpy as np
from jax import lax
from jax.experimental import pallas as pl
from jax.experimental.pallas import tpu as pltpu
from jax.sharding import PartitionSpec as P

CB = 128
NT = 4096
K0 = 8
HW = 64
R = 4
G = 16
BIN_DEV = 8
NB = 1024
NLAG = 2048
HALF = NB // 2
EPSILON = 1e-06
STEPS = 4
MESH = pl.DeviceIdType.MESH


def forward_factors():
    freqs = K0 + np.arange(NB)
    unit = 2.0 * math.pi / NT
    coarse = (np.arange(16)[:, None, None] * 64 * freqs[None, None, :]) % NT * unit
    fine = (np.arange(64)[:, None] * freqs[None, :]) % NT * unit
    tables = (np.cos(coarse), -np.sin(coarse), np.cos(fine), -np.sin(fine))
    return [jnp.asarray(t, jnp.float32) for t in tables]


def inverse_factors():
    unit = 2.0 * math.pi / NT
    freqs = K0 + np.arange(NB)
    fine = (freqs[:, None] * np.arange(128)[None, :] * 2) % NT * unit
    coarse = (freqs[None, :16] * (np.arange(16)[:, None] * 128 - NLAG // 2) * 2) % NT * unit
    fine = np.stack([np.cos(fine), np.sin(fine)]).reshape(2, 2, 4, 128, 128)
    coarse = np.stack([np.cos(coarse), np.sin(coarse)]) / math.sqrt(NB)
    coarse = np.broadcast_to(coarse[..., None], (2, 16, 16, 128))
    return [jnp.asarray(fine, jnp.float32), jnp.asarray(coarse, jnp.float32)]


def peer(c, r):
    x, y, z = c % 2, (c // 2) % 4, c // 8
    return ((z + r % 4) % 4) * 8 + ((y + (r // 4) % 4) % 4) * 2 + (x + r // 16) % 2


def loop(first, last, body):
    def step(n, carry):
        body(n)
        return carry

    lax.fori_loop(first, last, step, 0)


def stack_kernel(
    total_segs,
    traces, coarse_re, coarse_im, fine_re, fine_im, inv_fine, inv_coarse, info_ref,
    out_ref,
    x_ref, tab, spec, power, inv_level, valid_ref, send, recv, acc,
    fine_ref, inv_hi, inv_lo, info, onehot, scale_ref, raw, raw_in, bins, bins_in, part, part_in,
    x_sem, fine_sem, own_sem, send_sem, recv_sem,
    info_send, info_recv, raw_send, raw_recv, bins_send, bins_recv, part_send, part_recv,
):
    chans = lax.axis_size("chan")
    quarters = lax.axis_size("seg")
    me = lax.axis_index("chan")
    seg = lax.axis_index("seg")
    segs = x_ref.shape[0] // STEPS
    rows = segs * CB
    tiles = chans * R

    def load(i):
        part_of = pl.ds(i * segs, segs)
        return pltpu.make_async_copy(traces.at[part_of], x_ref.at[part_of], x_sem.at[i])

    def load_fine():
        return pltpu.make_async_copy(inv_fine.at[:, :, seg], fine_ref, fine_sem)

    for i in range(STEPS):
        load(i).start()
    load_fine().start()

    barrier = pltpu.get_barrier_semaphore()

    def greet(r):
        pl.semaphore_signal(barrier, inc=1, device_id={"chan": peer(me, r)}, device_id_type=MESH)

    def greet_seg(q):
        to = (seg + q) % quarters
        pl.semaphore_signal(barrier, inc=1, device_id={"seg": to}, device_id_type=MESH)

    loop(1, chans, greet)
    loop(1, quarters, greet_seg)

    turn = lax.broadcasted_iota(jnp.int32, (64, 128), 1) % 4
    c0 = jnp.where(turn == 0, 1.0, jnp.where(turn == 2, -1.0, 0.0)).astype(jnp.bfloat16)
    c1 = jnp.where(turn == 1, 1.0, jnp.where(turn == 3, -1.0, 0.0)).astype(jnp.bfloat16)
    flip = jnp.where(turn % 2 == 0, 1.0, -1.0).astype(jnp.bfloat16)

    def make_rows(a):
        for chunk in range(NB // 128):
            cols = pl.ds(chunk * 128, 128)
            ar, ai = coarse_re[a, :, cols], coarse_im[a, :, cols]
            br, bi = fine_re[:, cols], fine_im[:, cols]
            re = (ar * br - ai * bi).astype(jnp.bfloat16)
            im = (ar * bi + ai * br).astype(jnp.bfloat16)
            re1, im1 = re * c0 + im * c1, im * c0 - re * c1
            base = (chunk // 4) * NB + (chunk % 4) * 128
            for quarter, (u, v) in enumerate(
                ((re, im), (re1, im1), (re * flip, im * flip), (re1 * flip, im1 * flip))
            ):
                at = pl.ds(pl.multiple_of(quarter * 1024 + a * 64, 64), 64)
                tab[at, pl.ds(base, 128)] = u
                tab[at, pl.ds(base + HALF, 128)] = v

    loop(0, 16, make_rows)

    own = jnp.broadcast_to(info_ref[:, pl.ds(0, CB)].astype(jnp.float32), (CB, CB))
    diagonal = lax.broadcasted_iota(jnp.int32, (CB, CB), 0) == lax.broadcasted_iota(
        jnp.int32, (CB, CB), 1
    )
    column = jnp.sum(jnp.where(diagonal, own, 0.0), axis=1, keepdims=True)
    valid_ref[...] = jnp.broadcast_to(column, (CB, CB))

    power[:, pl.ds(0, 128)] = jnp.zeros((rows, 128), jnp.bfloat16)
    power[:, pl.ds(128 + NB, 128)] = jnp.zeros((rows, 128), jnp.bfloat16)
    near = (
        lax.broadcasted_iota(jnp.int32, (512, 256), 0)
        - lax.broadcasted_iota(jnp.int32, (512, 256), 1)
        - 128
    )
    band = jnp.where(jnp.abs(near) <= HW, 1.0, 0.0).astype(jnp.bfloat16)

    def exchange(i, r):
        to = peer(me, r)
        return pltpu.make_async_remote_copy(
            send.at[i, to // 2, to % 2],
            recv.at[i, me],
            send_sem.at[i, to],
            recv_sem.at[i, me],
            device_id={"chan": to},
            device_id_type=MESH,
        )

    def arrival(i, r):
        source = peer(me, r)
        return pltpu.make_async_copy(recv.at[i, source], recv.at[i, source], recv_sem.at[i, source])

    def keep(i):
        return pltpu.make_async_copy(send.at[i, me // 2, me % 2], recv.at[i, me], own_sem.at[i])

    def tell(r):
        to = peer(me, r)
        return pltpu.make_async_remote_copy(
            info_ref,
            info.at[me],
            info_send.at[to],
            info_recv.at[me],
            device_id={"chan": to},
            device_id_type=MESH,
        )

    def told(r):
        source = peer(me, r)
        return pltpu.make_async_copy(info.at[source], info.at[source], info_recv.at[source])

    pl.semaphore_wait(barrier, chans - 1 + quarters - 1)

    def whiten_step(i):
        load(i).wait()

        def transform(n):
            cols = pl.ds(pl.multiple_of(n * 256, 256), 256)
            block = x_ref[pl.ds(i * segs, segs)].reshape(rows, NT)
            spec[:, cols] = jnp.dot(block, tab[:, cols], preferred_element_type=jnp.float32)

        loop(0, 2 * NB // 256, transform)

        def add_power(n):
            at = pl.ds(pl.multiple_of(n * 32, 32), 32)
            for chunk in range(NB // 256):
                base = (chunk // 2) * NB + (chunk % 2) * 256
                re, im = spec[at, pl.ds(base, 256)], spec[at, pl.ds(base + HALF, 256)]
                power[at, pl.ds(128 + chunk * 256, 256)] = (re * re + im * im).astype(jnp.bfloat16)

        loop(0, rows // 32, add_power)

        for chunk in range(NB // 256):
            total = jnp.dot(
                power[:, pl.ds(chunk * 256, 512)], band, preferred_element_type=jnp.float32
            )
            k = chunk * 256 + lax.broadcasted_iota(jnp.int32, (1, 256), 1)
            count = jnp.minimum(k + HW, NB - 1) - jnp.maximum(k - HW, 0) + 1
            inv_level[:, pl.ds(chunk * 256, 256)] = lax.rsqrt(
                total * (1.0 / count.astype(jnp.float32)) + EPSILON
            )

        def scale(g):
            valid = valid_ref[pl.ds(pl.multiple_of(g * 8, 8), 8), :]
            for chunk in range(NB // 128):
                h, at = chunk // 4, (chunk % 4) * 128
                res, ims = [], []
                for s in range(segs):
                    row = pl.ds(pl.multiple_of(s * CB + g * 8, 8), 8)
                    weight = inv_level[row, pl.ds(chunk * 128, 128)] * valid
                    res.append(spec[row, pl.ds(h * NB + at, 128)] * weight)
                    ims.append(spec[row, pl.ds(h * NB + HALF + at, 128)] * weight)
                send[i, g, h, :, pl.ds(at, 128)] = jnp.concatenate(res, 0).astype(jnp.bfloat16)
                send[i, g, h, :, pl.ds(HALF + at, 128)] = jnp.concatenate(ims, 0).astype(jnp.bfloat16)

        loop(0, G, scale)
        keep(i).start()
        loop(1, chans, lambda r: exchange(i, r).start())

    loop(0, STEPS, whiten_step)
    loop(1, chans, lambda r: tell(r).start())

    recv[:, pl.ds(chans, R)] = jnp.zeros((STEPS, R, 8 * segs, NB), jnp.bfloat16)
    acc[...] = jnp.zeros_like(acc)
    load_fine().wait()

    def make_inverse(n):
        h, at = n // 8, pl.multiple_of((n % 8) * 16, 16)
        br, bi = fine_ref[0, h, pl.ds(at, 16)], fine_ref[1, h, pl.ds(at, 16)]
        for a in range(16):
            ar, ai = inv_coarse[0, a], inv_coarse[1, a]
            re, im = ar * br - ai * bi, -(ar * bi + ai * br)
            for which, value in enumerate((re, im)):
                at_row = pl.ds(pl.multiple_of(h * 256 + which * 128 + at, 16), 16)
                high = value.astype(jnp.bfloat16)
                inv_hi[at_row, pl.ds(a * 128, 128)] = high
                low = value - high.astype(jnp.float32)
                inv_lo[at_row, pl.ds(a * 128, 128)] = low.astype(jnp.bfloat16)

    loop(0, 16, make_inverse)

    def products(i, chunk, first):
        re_at = pl.ds(pl.multiple_of(chunk * 128, 128), 128)
        im_at = pl.ds(pl.multiple_of(HALF + chunk * 128, 128), 128)
        re = [recv[i, first + j, :, re_at].astype(jnp.float32) for j in range(4 + R)]
        im = [recv[i, first + j, :, im_at].astype(jnp.float32) for j in range(4 + R)]
        for j in range(4):
            for d in range(1, R + 1):
                p = re[j] * re[j + d] + im[j] * im[j + d]
                q = im[j] * re[j + d] - re[j] * im[j + d]
                t = (d - 1) * chans + first + j
                acc[chunk, t, :, pl.ds(0, 128)] += p.reshape(segs, 8, 128).sum(0)
                acc[chunk, t, :, pl.ds(128, 128)] += q.reshape(segs, 8, 128).sum(0)

    def all_here(i):
        loop(1, chans, lambda r: arrival(i, r).wait())
        keep(i).wait()

    def cross_step(i):
        all_here(i)
        loop(0, chans, lambda n: products(i, n % 4, (n // 4) * 4))

    loop(0, STEPS - 1, cross_step)

    info[pl.ds(me, 1)] = info_ref[...].reshape(1, 1, 256)
    info[pl.ds(chans, 8)] = jnp.zeros((8, 1, 256), jnp.int32)
    loop(1, chans, lambda r: told(r).wait())
    group = me // 2
    lanes = lax.broadcasted_iota(jnp.int32, (chans, CB), 1)
    everyone = info[...].reshape(chans + 8, 256).astype(jnp.float32)
    masks, names = everyone[:, :CB], everyone[:chans, CB:]
    picked = []
    for d in range(1, R + 1):
        both = masks[:chans] * masks[d : d + chans]
        count = jnp.sum(jnp.where(lanes // 8 == group, both, 0.0), axis=1, keepdims=True)
        factor = 1.0 / (total_segs * jnp.maximum(count, 1.0))
        scale_ref[pl.ds((d - 1) * chans, chans), :] = jnp.broadcast_to(factor, (chans, 256))
        mine = lanes == (d - 1) * G + group
        name = jnp.sum(jnp.where(mine, names, 0.0), axis=1, keepdims=True)
        bin_of = lax.broadcasted_iota(jnp.int32, (chans, 256), 1).astype(jnp.float32)
        picked.append(jnp.where(jnp.broadcast_to(name, (chans, 256)) == bin_of, 1.0, 0.0))
    onehot[...] = jnp.concatenate(picked, 0).T.astype(jnp.bfloat16)

    all_here(STEPS - 1)

    def hand_over(q):
        to = (seg + q) % quarters
        return pltpu.make_async_remote_copy(
            raw.at[to],
            raw_in.at[seg],
            raw_send.at[to],
            raw_recv.at[seg],
            device_id={"seg": to},
            device_id_type=MESH,
        )

    def finish_quarter(chunk):
        loop(0, chans // 4, lambda n: products(STEPS - 1, chunk, n * 4))

        def reduce_rows(n):
            at = pl.ds(pl.multiple_of(n * 8, 8), 8)
            raw[chunk, at, :] = acc[chunk, at].sum(1)

        loop(0, tiles // 8, reduce_rows)

    def give(q):
        finish_quarter((seg + q) % quarters)
        hand_over(q).start()

    loop(1, quarters, give)
    finish_quarter(seg)

    def got(q):
        source = (seg + q) % quarters
        pltpu.make_async_copy(raw_in.at[source], raw_in.at[source], raw_recv.at[source]).wait()

    loop(1, quarters, got)
    sums = raw[seg]
    for q in range(1, 4):
        sums = sums + raw_in[(seg + q) % quarters]
    sums = sums * scale_ref[...]
    high = sums.astype(jnp.bfloat16)
    low = (sums - high.astype(jnp.float32)).astype(jnp.bfloat16)
    stacked = jnp.dot(onehot[...], high, preferred_element_type=jnp.float32)
    stacked += jnp.dot(onehot[...], low, preferred_element_type=jnp.float32)
    bins[...] = stacked.reshape(chans, BIN_DEV, 256)

    def deliver(r):
        to = peer(me, r)
        return pltpu.make_async_remote_copy(
            bins.at[to],
            bins_in.at[me],
            bins_send.at[to],
            bins_recv.at[me],
            device_id={"chan": to},
            device_id_type=MESH,
        )

    loop(1, chans, lambda r: deliver(r).start())
    bins_in[me] = bins[me]

    def delivered(r):
        source = peer(me, r)
        pltpu.make_async_copy(bins_in.at[source], bins_in.at[source], bins_recv.at[source]).wait()

    loop(1, chans, delivered)
    halves = []
    for h in range(2):
        total = bins_in[h]
        for g in range(1, G):
            total = total + bins_in[2 * g + h]
        halves.append(total)
    spectra = jnp.concatenate(halves, axis=1)
    high = spectra.astype(jnp.bfloat16)
    low = (spectra - high.astype(jnp.float32)).astype(jnp.bfloat16)
    for n in range(NLAG // 512):
        cols = pl.ds(n * 512, 512)
        value = jnp.dot(high, inv_hi[:, cols], preferred_element_type=jnp.float32)
        value += jnp.dot(low, inv_hi[:, cols], preferred_element_type=jnp.float32)
        value += jnp.dot(high, inv_lo[:, cols], preferred_element_type=jnp.float32)
        part[:, cols] = value

    def share(q):
        to = (seg + q) % quarters
        return pltpu.make_async_remote_copy(
            part,
            part_in.at[seg],
            part_send.at[to],
            part_recv.at[seg],
            device_id={"seg": to},
            device_id_type=MESH,
        )

    loop(1, quarters, lambda q: share(q).start())

    def shared(q):
        source = (seg + q) % quarters
        pltpu.make_async_copy(part_in.at[source], part_in.at[source], part_recv.at[source]).wait()

    part_in[seg] = part[...]
    loop(1, quarters, shared)
    out_ref[...] = (part_in[0] + part_in[1]) + (part_in[2] + part_in[3])

    for i in range(STEPS):
        loop(1, chans, lambda r: exchange(i, r).wait_send())
    loop(1, chans, lambda r: tell(r).wait_send())
    loop(1, chans, lambda r: deliver(r).wait_send())
    loop(1, quarters, lambda q: hand_over(q).wait_send())
    loop(1, quarters, lambda q: share(q).wait_send())


def per_device(traces, channel_mask, owner_ids, local_bins):
    chans, quarters = lax.axis_size("chan"), lax.axis_size("seg")
    tiles = chans * R
    segs = traces.shape[0] // STEPS
    labels = owner_ids.reshape(1, -1) * BIN_DEV + local_bins
    info = jnp.concatenate([channel_mask.reshape(1, -1), labels, jnp.zeros_like(labels)], axis=1)
    vmem = pl.BlockSpec(memory_space=pltpu.VMEM)
    anywhere = pl.BlockSpec(memory_space=pl.ANY)
    dma = pltpu.SemaphoreType.DMA
    bf16, f32 = jnp.bfloat16, jnp.float32
    return pl.pallas_call(
        functools.partial(stack_kernel, float(traces.shape[0] * quarters)),
        out_shape=jax.ShapeDtypeStruct((BIN_DEV, NLAG), f32),
        in_specs=[anywhere] + [vmem] * 4 + [anywhere, vmem, vmem],
        out_specs=vmem,
        scratch_shapes=[
            pltpu.VMEM(traces.shape, bf16),
            pltpu.VMEM((NT, 2 * NB), bf16),
            pltpu.VMEM((segs * CB, 2 * NB), f32),
            pltpu.VMEM((segs * CB, NB + 256), bf16),
            pltpu.VMEM((segs * CB, NB), f32),
            pltpu.VMEM((CB, CB), f32),
            pltpu.VMEM((STEPS, G, 2, 8 * segs, NB), bf16),
            pltpu.VMEM((STEPS, chans + R, 8 * segs, NB), bf16),
            pltpu.VMEM((4, tiles, 8, 256), f32),
            pltpu.VMEM((2, 2, 128, 128), f32),
            pltpu.VMEM((512, NLAG), bf16),
            pltpu.VMEM((512, NLAG), bf16),
            pltpu.VMEM((chans + 8, 1, 256), jnp.int32),
            pltpu.VMEM((256, tiles), bf16),
            pltpu.VMEM((tiles, 256), f32),
            pltpu.VMEM((4, tiles, 256), f32),
            pltpu.VMEM((4, tiles, 256), f32),
            pltpu.VMEM((chans, BIN_DEV, 256), f32),
            pltpu.VMEM((chans, BIN_DEV, 256), f32),
            pltpu.VMEM((BIN_DEV, NLAG), f32),
            pltpu.VMEM((4, BIN_DEV, NLAG), f32),
            dma((STEPS,)), dma, dma((STEPS,)), dma((STEPS, chans)), dma((STEPS, chans)),
            dma((chans,)), dma((chans,)), dma((4,)), dma((4,)),
            dma((chans,)), dma((chans,)), dma((4,)), dma((4,)),
        ],
        compiler_params=pltpu.CompilerParams(
            collective_id=0, has_side_effects=True, vmem_limit_bytes=60 << 20
        ),
        name="stack",
    )(traces, *forward_factors(), *inverse_factors(), info)


def solution(mesh):
    in_specs = (P("seg", "chan", None), P("chan"), P("chan", None, None), P("chan", None))
    return jax.shard_map(
        per_device, mesh=mesh, in_specs=in_specs, out_specs=P("chan", None), check_vma=False
    )
```

```python
import functools
import math

import jax
import jax.numpy as jnp
import numpy as np
from jax import lax
from jax.experimental import pallas as pl
from jax.experimental.pallas import tpu as pltpu
from jax.sharding import PartitionSpec as P

CB = 128
NT = 4096
K0 = 8
HW = 64
R = 4
G = 16
BIN_DEV = 8
NB = 1024
NLAG = 2048
HALF = NB // 2
EPSILON = 1e-06
STEPS = 4
MESH = pl.DeviceIdType.MESH


def forward_factors():
    freqs = K0 + np.arange(NB)
    unit = 2.0 * math.pi / NT
    coarse = (np.arange(16)[:, None, None] * 64 * freqs[None, None, :]) % NT * unit
    fine = (np.arange(64)[:, None] * freqs[None, :]) % NT * unit
    tables = (np.cos(coarse), -np.sin(coarse), np.cos(fine), -np.sin(fine))
    return [jnp.asarray(t, jnp.float32) for t in tables]


def inverse_factors():
    unit = 2.0 * math.pi / NT
    freqs = K0 + np.arange(NB)
    fine = (freqs[:, None] * np.arange(128)[None, :] * 2) % NT * unit
    coarse = (freqs[None, :16] * (np.arange(16)[:, None] * 128 - NLAG // 2) * 2) % NT * unit
    fine = np.stack([np.cos(fine), np.sin(fine)]).reshape(2, 2, 4, 128, 128)
    coarse = np.stack([np.cos(coarse), np.sin(coarse)]) / math.sqrt(NB)
    coarse = np.broadcast_to(coarse[..., None], (2, 16, 16, 128))
    return [jnp.asarray(fine, jnp.float32), jnp.asarray(coarse, jnp.float32)]


def peer(c, r):
    x, y, z = c % 2, (c // 2) % 4, c // 8
    return ((z + r % 4) % 4) * 8 + ((y + (r // 4) % 4) % 4) * 2 + (x + r // 16) % 2


def loop(first, last, body):
    def step(n, carry):
        body(n)
        return carry

    lax.fori_loop(first, last, step, 0)


def stack_kernel(
    total_segs,
    traces, coarse_re, coarse_im, fine_re, fine_im, inv_fine, inv_coarse, info_ref,
    out_ref,
    x_ref, tab, spec, power, inv_level, valid_ref, send, recv, acc,
    fine_ref, inv_hi, inv_lo, info, onehot, scale_ref, raw, raw_in, half, half_in,
    bins, bins_in, part, part_in,
    x_sem, fine_sem, own_sem, send_sem, recv_sem, info_send, info_recv, raw_send, raw_recv,
    half_send, half_recv, bins_send, bins_recv, part_send, part_recv,
):
    chans = lax.axis_size("chan")
    me = lax.axis_index("chan")
    seg = lax.axis_index("seg")
    other_core = seg + 1 - 2 * (seg % 2)
    other_chip = (seg + 2) % 4
    segs = x_ref.shape[0] // STEPS
    rows = segs * CB
    tiles = chans * R

    def load(i):
        part_of = pl.ds(i * segs, segs)
        return pltpu.make_async_copy(traces.at[part_of], x_ref.at[part_of], x_sem.at[i])

    def load_fine():
        return pltpu.make_async_copy(inv_fine.at[:, :, seg], fine_ref, fine_sem)

    for i in range(STEPS):
        load(i).start()
    load_fine().start()

    barrier = pltpu.get_barrier_semaphore()

    def greet(r):
        pl.semaphore_signal(barrier, inc=1, device_id={"chan": peer(me, r)}, device_id_type=MESH)

    for to in (other_core, other_chip):
        pl.semaphore_signal(barrier, inc=1, device_id={"seg": to}, device_id_type=MESH)
    loop(1, chans, greet)

    turn = lax.broadcasted_iota(jnp.int32, (64, 128), 1) % 4
    c0 = jnp.where(turn == 0, 1.0, jnp.where(turn == 2, -1.0, 0.0)).astype(jnp.bfloat16)
    c1 = jnp.where(turn == 1, 1.0, jnp.where(turn == 3, -1.0, 0.0)).astype(jnp.bfloat16)
    flip = jnp.where(turn % 2 == 0, 1.0, -1.0).astype(jnp.bfloat16)

    def make_rows(a):
        for chunk in range(NB // 128):
            cols = pl.ds(chunk * 128, 128)
            ar, ai = coarse_re[a, :, cols], coarse_im[a, :, cols]
            br, bi = fine_re[:, cols], fine_im[:, cols]
            re = (ar * br - ai * bi).astype(jnp.bfloat16)
            im = (ar * bi + ai * br).astype(jnp.bfloat16)
            re1, im1 = re * c0 + im * c1, im * c0 - re * c1
            base = (chunk // 4) * NB + (chunk % 4) * 128
            for quarter, (u, v) in enumerate(
                ((re, im), (re1, im1), (re * flip, im * flip), (re1 * flip, im1 * flip))
            ):
                at = pl.ds(pl.multiple_of(quarter * 1024 + a * 64, 64), 64)
                tab[at, pl.ds(base, 128)] = u
                tab[at, pl.ds(base + HALF, 128)] = v

    loop(0, 16, make_rows)

    own = jnp.broadcast_to(info_ref[:, pl.ds(0, CB)].astype(jnp.float32), (CB, CB))
    diagonal = lax.broadcasted_iota(jnp.int32, (CB, CB), 0) == lax.broadcasted_iota(
        jnp.int32, (CB, CB), 1
    )
    column = jnp.sum(jnp.where(diagonal, own, 0.0), axis=1, keepdims=True)
    valid_ref[...] = jnp.broadcast_to(column, (CB, CB))

    power[:, pl.ds(0, 128)] = jnp.zeros((rows, 128), jnp.bfloat16)
    power[:, pl.ds(128 + NB, 128)] = jnp.zeros((rows, 128), jnp.bfloat16)
    near = (
        lax.broadcasted_iota(jnp.int32, (512, 256), 0)
        - lax.broadcasted_iota(jnp.int32, (512, 256), 1)
        - 128
    )
    band = jnp.where(jnp.abs(near) <= HW, 1.0, 0.0).astype(jnp.bfloat16)

    def exchange(i, r):
        to = peer(me, r)
        return pltpu.make_async_remote_copy(
            send.at[i, to],
            recv.at[i, me],
            send_sem.at[i],
            recv_sem.at[i],
            device_id={"chan": to},
            device_id_type=MESH,
        )

    def await_all(ref, sem):
        pieces = ref.at[pl.ds(0, chans - 1)]
        pltpu.make_async_copy(pieces, pieces, sem).wait()

    def keep(i):
        return pltpu.make_async_copy(send.at[i, me], recv.at[i, me], own_sem.at[i])

    def tell(r):
        to = peer(me, r)
        return pltpu.make_async_remote_copy(
            info_ref,
            info.at[me],
            info_send,
            info_recv,
            device_id={"chan": to},
            device_id_type=MESH,
        )

    def whiten_step(i):
        load(i).wait()

        def transform(n):
            cols = pl.ds(pl.multiple_of(n * 256, 256), 256)
            block = x_ref[pl.ds(i * segs, segs)].reshape(rows, NT)
            spec[:, cols] = jnp.dot(block, tab[:, cols], preferred_element_type=jnp.float32)

        loop(0, 2 * NB // 256, transform)

        def add_power(n):
            at = pl.ds(pl.multiple_of(n * 32, 32), 32)
            for chunk in range(NB // 256):
                base = (chunk // 2) * NB + (chunk % 2) * 256
                re, im = spec[at, pl.ds(base, 256)], spec[at, pl.ds(base + HALF, 256)]
                power[at, pl.ds(128 + chunk * 256, 256)] = (re * re + im * im).astype(jnp.bfloat16)

        loop(0, rows // 32, add_power)

        for chunk in range(NB // 256):
            total = jnp.dot(
                power[:, pl.ds(chunk * 256, 512)], band, preferred_element_type=jnp.float32
            )
            k = chunk * 256 + lax.broadcasted_iota(jnp.int32, (1, 256), 1)
            count = jnp.minimum(k + HW, NB - 1) - jnp.maximum(k - HW, 0) + 1
            inv_level[:, pl.ds(chunk * 256, 256)] = lax.rsqrt(
                total * (1.0 / count.astype(jnp.float32)) + EPSILON
            )

        def scale(g):
            valid = valid_ref[pl.ds(pl.multiple_of(g * 8, 8), 8), :]
            for chunk in range(NB // 128):
                h, at = chunk // 4, (chunk % 4) * 128
                res, ims = [], []
                for s in range(segs):
                    row = pl.ds(pl.multiple_of(s * CB + g * 8, 8), 8)
                    weight = inv_level[row, pl.ds(chunk * 128, 128)] * valid
                    res.append(spec[row, pl.ds(h * NB + at, 128)] * weight)
                    ims.append(spec[row, pl.ds(h * NB + HALF + at, 128)] * weight)
                send[i, 2 * g + h, :, pl.ds(at, 128)] = jnp.concatenate(res, 0).astype(jnp.bfloat16)
                send[i, 2 * g + h, :, pl.ds(HALF + at, 128)] = jnp.concatenate(ims, 0).astype(jnp.bfloat16)

        loop(0, G, scale)
        keep(i).start()

    def send_step(i):
        loop(1, chans, lambda r: exchange(i, r).start())

    def later_step(i):
        whiten_step(i)
        send_step(i)

    whiten_step(0)
    pl.semaphore_wait(barrier, chans + 1)
    send_step(0)
    loop(1, chans, lambda r: tell(r).start())
    loop(1, STEPS, later_step)

    recv[:, pl.ds(chans, R)] = jnp.zeros((STEPS, R, 8 * segs, NB), jnp.bfloat16)
    load_fine().wait()

    def make_inverse(n):
        h, at = n // 8, pl.multiple_of((n % 8) * 16, 16)
        br, bi = fine_ref[0, h, pl.ds(at, 16)], fine_ref[1, h, pl.ds(at, 16)]
        for a in range(16):
            ar, ai = inv_coarse[0, a], inv_coarse[1, a]
            re, im = ar * br - ai * bi, -(ar * bi + ai * br)
            for which, value in enumerate((re, im)):
                at_row = pl.ds(pl.multiple_of(h * 256 + which * 128 + at, 16), 16)
                high = value.astype(jnp.bfloat16)
                inv_hi[at_row, pl.ds(a * 128, 128)] = high
                low = value - high.astype(jnp.float32)
                inv_lo[at_row, pl.ds(a * 128, 128)] = low.astype(jnp.bfloat16)

    loop(0, 16, make_inverse)

    def products(i, chunk, first, add=True):
        re_at = pl.ds(pl.multiple_of(chunk * 128, 128), 128)
        im_at = pl.ds(pl.multiple_of(HALF + chunk * 128, 128), 128)
        re = [recv[i, first + j, :, re_at].astype(jnp.float32) for j in range(4 + R)]
        im = [recv[i, first + j, :, im_at].astype(jnp.float32) for j in range(4 + R)]
        for j in range(4):
            for d in range(1, R + 1):
                p = re[j] * re[j + d] + im[j] * im[j + d]
                q = im[j] * re[j + d] - re[j] * im[j + d]
                t = (d - 1) * chans + first + j
                p, q = p.reshape(segs, 8, 128).sum(0), q.reshape(segs, 8, 128).sum(0)
                if add:
                    p = p + acc[chunk, t, :, pl.ds(0, 128)]
                    q = q + acc[chunk, t, :, pl.ds(128, 128)]
                acc[chunk, t, :, pl.ds(0, 128)] = p
                acc[chunk, t, :, pl.ds(128, 128)] = q

    def all_here(i):
        await_all(recv.at[i], recv_sem.at[i])
        keep(i).wait()

    def cross_step(i):
        all_here(i)
        loop(0, chans, lambda n: products(i, n % 4, (n // 4) * 4))

    all_here(0)
    loop(0, chans, lambda n: products(0, n % 4, (n // 4) * 4, add=False))
    loop(1, STEPS - 1, cross_step)

    info[pl.ds(me, 1)] = info_ref[...].reshape(1, 1, 256)
    info[pl.ds(chans, 8)] = jnp.zeros((8, 1, 256), jnp.int32)
    await_all(info, info_recv)
    group = me // 2
    lanes = lax.broadcasted_iota(jnp.int32, (chans, CB), 1)
    everyone = info[...].reshape(chans + 8, 256).astype(jnp.float32)
    masks, names = everyone[:, :CB], everyone[:chans, CB:]
    picked = []
    for d in range(1, R + 1):
        both = masks[:chans] * masks[d : d + chans]
        count = jnp.sum(jnp.where(lanes // 8 == group, both, 0.0), axis=1, keepdims=True)
        factor = 1.0 / (total_segs * jnp.maximum(count, 1.0))
        scale_ref[pl.ds((d - 1) * chans, chans), :] = jnp.broadcast_to(factor, (chans, 256))
        mine = lanes == (d - 1) * G + group
        name = jnp.sum(jnp.where(mine, names, 0.0), axis=1, keepdims=True)
        bin_of = lax.broadcasted_iota(jnp.int32, (chans, 256), 1).astype(jnp.float32)
        picked.append(jnp.where(jnp.broadcast_to(name, (chans, 256)) == bin_of, 1.0, 0.0))
    onehot[...] = jnp.concatenate(picked, 0).T.astype(jnp.bfloat16)

    all_here(STEPS - 1)

    def hand_over(n, chunk):
        return pltpu.make_async_remote_copy(
            raw.at[chunk],
            raw_in.at[n],
            raw_send.at[n],
            raw_recv.at[n],
            device_id={"seg": other_core},
            device_id_type=MESH,
        )

    def finish_quarter(chunk):
        loop(0, chans // 4, lambda n: products(STEPS - 1, chunk, n * 4))

        def reduce_rows(n):
            at = pl.ds(pl.multiple_of(n * 8, 8), 8)
            raw[chunk, at, :] = acc[chunk, at].sum(1)

        loop(0, tiles // 8, reduce_rows)

    chip = seg - seg % 2
    far = 2 - chip

    def give(n):
        chunk = jnp.where(n == 0, far, chip) + other_core % 2
        finish_quarter(chunk)
        hand_over(n, chunk).start()

    loop(0, 2, give)
    cross_chip = pltpu.make_async_remote_copy(
        half, half_in, half_send, half_recv, device_id={"seg": other_chip}, device_id_type=MESH
    )
    finish_quarter(other_chip)
    hand_over(0, far + other_core % 2).wait()
    half[...] = (raw[other_chip] + raw_in[0]).astype(jnp.bfloat16)
    cross_chip.start()
    finish_quarter(seg)
    hand_over(1, other_core).wait()
    cross_chip.wait()
    sums = raw[seg] + raw_in[1] + half_in[...].astype(jnp.float32)
    sums = sums * scale_ref[...]
    high = sums.astype(jnp.bfloat16)
    low = (sums - high.astype(jnp.float32)).astype(jnp.bfloat16)
    stacked = jnp.dot(onehot[...], high, preferred_element_type=jnp.float32)
    stacked += jnp.dot(onehot[...], low, preferred_element_type=jnp.float32)
    bins[...] = stacked.reshape(chans, BIN_DEV, 256).astype(jnp.bfloat16)

    def deliver(r):
        to = peer(me, r)
        return pltpu.make_async_remote_copy(
            bins.at[to],
            bins_in.at[me],
            bins_send,
            bins_recv,
            device_id={"chan": to},
            device_id_type=MESH,
        )

    loop(1, chans, lambda r: deliver(r).start())
    bins_in[me] = bins[me]
    await_all(bins_in, bins_recv)
    halves = []
    for h in range(2):
        total = bins_in[h].astype(jnp.float32)
        for g in range(1, G):
            total = total + bins_in[2 * g + h].astype(jnp.float32)
        halves.append(total)
    spectra = jnp.concatenate(halves, axis=1)
    high = spectra.astype(jnp.bfloat16)
    low = (spectra - high.astype(jnp.float32)).astype(jnp.bfloat16)
    for n in range(NLAG // 512):
        cols = pl.ds(n * 512, 512)
        value = jnp.dot(high, inv_hi[:, cols], preferred_element_type=jnp.float32)
        value += jnp.dot(low, inv_hi[:, cols], preferred_element_type=jnp.float32)
        value += jnp.dot(high, inv_lo[:, cols], preferred_element_type=jnp.float32)
        part[0, :, cols] = value

    def share(n, to):
        return pltpu.make_async_remote_copy(
            part.at[n],
            part_in.at[n],
            part_send.at[n],
            part_recv.at[n],
            device_id={"seg": to},
            device_id_type=MESH,
        )

    share(0, other_core).start()
    share(0, other_core).wait()
    part[1] = part[0] + part_in[0]
    share(1, other_chip).start()
    share(1, other_chip).wait()
    out_ref[...] = part[1] + part_in[1]

    for i in range(STEPS):
        await_all(send.at[i], send_sem.at[i])
    await_all(info, info_send)
    await_all(bins_in, bins_send)


def per_device(traces, channel_mask, owner_ids, local_bins):
    chans, quarters = lax.axis_size("chan"), lax.axis_size("seg")
    tiles = chans * R
    segs = traces.shape[0] // STEPS
    labels = owner_ids.reshape(1, -1) * BIN_DEV + local_bins
    info = jnp.concatenate([channel_mask.reshape(1, -1), labels, jnp.zeros_like(labels)], axis=1)
    vmem = pl.BlockSpec(memory_space=pltpu.VMEM)
    anywhere = pl.BlockSpec(memory_space=pl.ANY)
    dma = pltpu.SemaphoreType.DMA
    bf16, f32 = jnp.bfloat16, jnp.float32
    return pl.pallas_call(
        functools.partial(stack_kernel, float(traces.shape[0] * quarters)),
        out_shape=jax.ShapeDtypeStruct((BIN_DEV, NLAG), f32),
        in_specs=[anywhere] + [vmem] * 4 + [anywhere, vmem, vmem],
        out_specs=vmem,
        scratch_shapes=[
            pltpu.VMEM(traces.shape, bf16),
            pltpu.VMEM((NT, 2 * NB), bf16),
            pltpu.VMEM((segs * CB, 2 * NB), f32),
            pltpu.VMEM((segs * CB, NB + 256), bf16),
            pltpu.VMEM((segs * CB, NB), f32),
            pltpu.VMEM((CB, CB), f32),
            pltpu.VMEM((STEPS, chans, 8 * segs, NB), bf16),
            pltpu.VMEM((STEPS, chans + R, 8 * segs, NB), bf16),
            pltpu.VMEM((4, tiles, 8, 256), f32),
            pltpu.VMEM((2, 2, 128, 128), f32),
            pltpu.VMEM((512, NLAG), bf16),
            pltpu.VMEM((512, NLAG), bf16),
            pltpu.VMEM((chans + 8, 1, 256), jnp.int32),
            pltpu.VMEM((256, tiles), bf16),
            pltpu.VMEM((tiles, 256), f32),
            pltpu.VMEM((4, tiles, 256), f32),
            pltpu.VMEM((2, tiles, 256), f32),
            pltpu.VMEM((tiles, 256), bf16),
            pltpu.VMEM((tiles, 256), bf16),
            pltpu.VMEM((chans, BIN_DEV, 256), bf16),
            pltpu.VMEM((chans, BIN_DEV, 256), bf16),
            pltpu.VMEM((2, BIN_DEV, NLAG), f32),
            pltpu.VMEM((2, BIN_DEV, NLAG), f32),
            dma((STEPS,)), dma, dma((STEPS,)), dma((STEPS,)), dma((STEPS,)),
            dma, dma, dma((2,)), dma((2,)), dma, dma, dma, dma, dma((2,)), dma((2,)),
        ],
        compiler_params=pltpu.CompilerParams(
            collective_id=0, has_side_effects=True, vmem_limit_bytes=60 << 20
        ),
        name="stack",
    )(traces, *forward_factors(), *inverse_factors(), info)


def solution(mesh):
    in_specs = (P("seg", "chan", None), P("chan"), P("chan", None, None), P("chan", None))
    return jax.shard_map(
        per_device, mesh=mesh, in_specs=in_specs, out_specs=P("chan", None), check_vma=False
    )
```

```python
import functools
import math

import jax
import jax.numpy as jnp
import numpy as np
from jax import lax
from jax.experimental import pallas as pl
from jax.experimental.pallas import tpu as pltpu
from jax.sharding import PartitionSpec as P

CB = 128
NT = 4096
K0 = 8
HW = 64
R = 4
G = 16
BIN_DEV = 8
NB = 1024
NLAG = 2048
HALF = NB // 2
EPSILON = 1e-06
STEPS = ((0, 1), (1, 1), (2, 2), (4, 2), (6, 2))
MESH = pl.DeviceIdType.MESH


def forward_factors():
    freqs = K0 + np.arange(NB)
    unit = 2.0 * math.pi / NT
    coarse = (np.arange(16)[:, None, None] * 64 * freqs[None, None, :]) % NT * unit
    fine = (np.arange(64)[:, None] * freqs[None, :]) % NT * unit
    tables = (np.cos(coarse), -np.sin(coarse), np.cos(fine), -np.sin(fine))
    return [jnp.asarray(t, jnp.float32) for t in tables]


def inverse_factors():
    unit = 2.0 * math.pi / NT
    freqs = K0 + np.arange(NB)
    fine = (freqs[:, None] * np.arange(128)[None, :] * 2) % NT * unit
    coarse = (freqs[None, :16] * (np.arange(16)[:, None] * 128 - NLAG // 2) * 2) % NT * unit
    fine = np.stack([np.cos(fine), np.sin(fine)]).reshape(2, 2, 4, 128, 128)
    coarse = np.stack([np.cos(coarse), np.sin(coarse)]) / math.sqrt(NB)
    coarse = np.broadcast_to(coarse[..., None], (2, 16, 16, 128))
    return [jnp.asarray(fine, jnp.float32), jnp.asarray(coarse, jnp.float32)]


def peer(c, r):
    x, y, z = c % 2, (c // 2) % 4, c // 8
    return ((z + r % 4) % 4) * 8 + ((y + (r // 4) % 4) % 4) * 2 + (x + r // 16) % 2


def loop(first, last, body):
    def step(n, carry):
        body(n)
        return carry

    lax.fori_loop(first, last, step, 0)


def stack_kernel(
    total_segs,
    traces, coarse_re, coarse_im, fine_re, fine_im, inv_fine, inv_coarse, mask_row, owners, locals_,
    out_ref,
    x_ref, tab, spec, power, inv_level, valid_ref, send_one, recv_one, send_two, recv_two, acc,
    info_ref, fine_ref, inv_hi, inv_lo, info, onehot, scale_ref, raw, raw_in, half, half_in,
    bins, bins_in, part, part_in,
    x_sem, fine_sem, own_sem, send_sem, recv_sem, info_send, info_recv, raw_send, raw_recv,
    half_send, half_recv, bins_send, bins_recv, part_send, part_recv,
):
    chans = lax.axis_size("chan")
    me = lax.axis_index("chan")
    seg = lax.axis_index("seg")
    other_core = seg + 1 - 2 * (seg % 2)
    other_chip = (seg + 2) % 4
    tiles = chans * R

    def load(i):
        at = pl.ds(*STEPS[i])
        return pltpu.make_async_copy(traces.at[at], x_ref.at[at], x_sem.at[i])

    def load_fine():
        return pltpu.make_async_copy(inv_fine.at[:, :, seg], fine_ref, fine_sem)

    for i in range(len(STEPS)):
        load(i).start()
    load_fine().start()
    info_ref[:, pl.ds(0, CB)] = mask_row[...]
    info_ref[:, pl.ds(CB, CB)] = jnp.zeros((1, CB), jnp.int32)
    info_ref[:, pl.ds(CB, R * G)] = owners[...] * BIN_DEV + locals_[...]

    barrier = pltpu.get_barrier_semaphore()

    def greet(r):
        pl.semaphore_signal(barrier, inc=1, device_id={"chan": peer(me, r)}, device_id_type=MESH)

    for to in (other_core, other_chip):
        pl.semaphore_signal(barrier, inc=1, device_id={"seg": to}, device_id_type=MESH)
    loop(1, chans, greet)

    turn = lax.broadcasted_iota(jnp.int32, (64, 128), 1) % 4
    c0 = jnp.where(turn == 0, 1.0, jnp.where(turn == 2, -1.0, 0.0)).astype(jnp.bfloat16)
    c1 = jnp.where(turn == 1, 1.0, jnp.where(turn == 3, -1.0, 0.0)).astype(jnp.bfloat16)
    flip = jnp.where(turn % 2 == 0, 1.0, -1.0).astype(jnp.bfloat16)

    def make_rows(a):
        for chunk in range(NB // 128):
            cols = pl.ds(chunk * 128, 128)
            ar, ai = coarse_re[a, :, cols], coarse_im[a, :, cols]
            br, bi = fine_re[:, cols], fine_im[:, cols]
            re = (ar * br - ai * bi).astype(jnp.bfloat16)
            im = (ar * bi + ai * br).astype(jnp.bfloat16)
            re1, im1 = re * c0 + im * c1, im * c0 - re * c1
            base = (chunk // 4) * NB + (chunk % 4) * 128
            for quarter, (u, v) in enumerate(
                ((re, im), (re1, im1), (re * flip, im * flip), (re1 * flip, im1 * flip))
            ):
                at = pl.ds(pl.multiple_of(quarter * 1024 + a * 64, 64), 64)
                tab[at, pl.ds(base, 128)] = u
                tab[at, pl.ds(base + HALF, 128)] = v

    loop(0, 16, make_rows)

    own = jnp.broadcast_to(info_ref[:, pl.ds(0, CB)].astype(jnp.float32), (CB, CB))
    diagonal = lax.broadcasted_iota(jnp.int32, (CB, CB), 0) == lax.broadcasted_iota(
        jnp.int32, (CB, CB), 1
    )
    column = jnp.sum(jnp.where(diagonal, own, 0.0), axis=1, keepdims=True)
    valid_ref[...] = jnp.broadcast_to(column, (CB, CB))

    power[:, pl.ds(0, 128)] = jnp.zeros((2 * CB, 128), jnp.bfloat16)
    power[:, pl.ds(128 + NB, 128)] = jnp.zeros((2 * CB, 128), jnp.bfloat16)
    near = (
        lax.broadcasted_iota(jnp.int32, (512, 256), 0)
        - lax.broadcasted_iota(jnp.int32, (512, 256), 1)
        - 128
    )
    band = jnp.where(jnp.abs(near) <= HW, 1.0, 0.0).astype(jnp.bfloat16)

    send = [send_one.at[0], send_one.at[1]] + [send_two.at[i] for i in range(3)]
    recv = [recv_one.at[0], recv_one.at[1]] + [recv_two.at[i] for i in range(3)]

    def exchange(i, r):
        to = peer(me, r)
        return pltpu.make_async_remote_copy(
            send[i].at[to],
            recv[i].at[me],
            send_sem.at[i],
            recv_sem.at[i],
            device_id={"chan": to},
            device_id_type=MESH,
        )

    def keep(i):
        return pltpu.make_async_copy(send[i].at[me], recv[i].at[me], own_sem.at[i])

    def await_all(ref, sem):
        pieces = ref.at[pl.ds(0, chans - 1)]
        pltpu.make_async_copy(pieces, pieces, sem).wait()

    def tell(r):
        to = peer(me, r)
        return pltpu.make_async_remote_copy(
            info_ref,
            info.at[me],
            info_send,
            info_recv,
            device_id={"chan": to},
            device_id_type=MESH,
        )

    def await_step(ref, i, sem):
        pieces = ref[i].at[pl.ds(0, chans - 1)]
        pltpu.make_async_copy(pieces, pieces, sem.at[i]).wait()

    def whiten_step(i):
        first, segs = STEPS[i]
        rows = segs * CB
        every = pl.ds(0, rows)
        load(i).wait()

        def transform(n):
            cols = pl.ds(pl.multiple_of(n * 512, 512), 512)
            block = x_ref[pl.ds(first, segs)].reshape(rows, NT)
            spec[every, cols] = jnp.dot(block, tab[:, cols], preferred_element_type=jnp.float32)

        loop(0, 2 * NB // 512, transform)

        def add_power(n):
            at = pl.ds(pl.multiple_of(n * 32, 32), 32)
            for chunk in range(NB // 256):
                base = (chunk // 2) * NB + (chunk % 2) * 256
                re, im = spec[at, pl.ds(base, 256)], spec[at, pl.ds(base + HALF, 256)]
                power[at, pl.ds(128 + chunk * 256, 256)] = (re * re + im * im).astype(jnp.bfloat16)

        loop(0, rows // 32, add_power)

        for chunk in range(NB // 256):
            total = jnp.dot(
                power[every, pl.ds(chunk * 256, 512)], band, preferred_element_type=jnp.float32
            )
            k = chunk * 256 + lax.broadcasted_iota(jnp.int32, (1, 256), 1)
            count = jnp.minimum(k + HW, NB - 1) - jnp.maximum(k - HW, 0) + 1
            inv_level[every, pl.ds(chunk * 256, 256)] = lax.rsqrt(
                total * (1.0 / count.astype(jnp.float32)) + EPSILON
            )

        def scale(g):
            valid = valid_ref[pl.ds(pl.multiple_of(g * 8, 8), 8), :]
            for s in range(segs):
                row = pl.ds(pl.multiple_of(s * CB + g * 8, 8), 8)
                for chunk in range(NB // 128):
                    h, at = chunk // 4, (chunk % 4) * 128
                    weight = inv_level[row, pl.ds(chunk * 128, 128)] * valid
                    re = spec[row, pl.ds(h * NB + at, 128)] * weight
                    im = spec[row, pl.ds(h * NB + HALF + at, 128)] * weight
                    to = 2 * g + h
                    block = send[i].at[to, s] if segs == 2 else send[i].at[to]
                    block[:, pl.ds(at, 128)] = re.astype(jnp.bfloat16)
                    block[:, pl.ds(HALF + at, 128)] = im.astype(jnp.bfloat16)

        loop(0, G, scale)
        keep(i).start()

    def send_step(i):
        loop(1, chans, lambda r: exchange(i, chans - r).start())

    whiten_step(0)
    pl.semaphore_wait(barrier, chans + 1)
    send_step(0)
    for i in range(1, len(STEPS)):
        whiten_step(i)
        send_step(i)
        if i == 2:
            loop(1, chans, lambda r: tell(r).start())

    for block in recv:
        block[pl.ds(chans, R)] = jnp.zeros((R,) + block.shape[1:], jnp.bfloat16)
    load_fine().wait()

    def make_inverse(n):
        h, at = n // 8, pl.multiple_of((n % 8) * 16, 16)
        br, bi = fine_ref[0, h, pl.ds(at, 16)], fine_ref[1, h, pl.ds(at, 16)]
        for a in range(16):
            ar, ai = inv_coarse[0, a], inv_coarse[1, a]
            re, im = ar * br - ai * bi, -(ar * bi + ai * br)
            for which, value in enumerate((re, im)):
                at_row = pl.ds(pl.multiple_of(h * 256 + which * 128 + at, 16), 16)
                high = value.astype(jnp.bfloat16)
                inv_hi[at_row, pl.ds(a * 128, 128)] = high
                low = value - high.astype(jnp.float32)
                inv_lo[at_row, pl.ds(a * 128, 128)] = low.astype(jnp.bfloat16)

    loop(0, 16, make_inverse)

    def products(pair, chunk, first, add=True):
        re_at = pl.ds(pl.multiple_of(chunk * 128, 128), 128)
        im_at = pl.ds(pl.multiple_of(HALF + chunk * 128, 128), 128)

        def part_of(j, s, at):
            block = recv[s].at[first + j] if pair == 0 else recv[pair + 1].at[first + j, s]
            return block[:, at].astype(jnp.float32)

        re = [[part_of(j, s, re_at) for j in range(4 + R)] for s in range(2)]
        im = [[part_of(j, s, im_at) for j in range(4 + R)] for s in range(2)]
        for j in range(4):
            for d in range(1, R + 1):
                t = (d - 1) * chans + first + j
                p = re[0][j] * re[0][j + d] + im[0][j] * im[0][j + d]
                q = im[0][j] * re[0][j + d] - re[0][j] * im[0][j + d]
                p += re[1][j] * re[1][j + d] + im[1][j] * im[1][j + d]
                q += im[1][j] * re[1][j + d] - re[1][j] * im[1][j + d]
                if add:
                    p = p + acc[chunk, t, :, pl.ds(0, 128)]
                    q = q + acc[chunk, t, :, pl.ds(128, 128)]
                acc[chunk, t, :, pl.ds(0, 128)] = p
                acc[chunk, t, :, pl.ds(128, 128)] = q

    def here(i):
        await_step(recv, i, recv_sem)
        keep(i).wait()

    here(0)
    here(1)
    loop(0, chans, lambda n: products(0, n % 4, (n // 4) * 4, add=False))
    for i in (2, 3):
        here(i)
        loop(0, chans, lambda n: products(i - 1, n % 4, (n // 4) * 4))

    info[pl.ds(me, 1)] = info_ref[...].reshape(1, 1, 256)
    info[pl.ds(chans, 8)] = jnp.zeros((8, 1, 256), jnp.int32)
    await_all(info, info_recv)
    group = me // 2
    lanes = lax.broadcasted_iota(jnp.int32, (chans, CB), 1)
    everyone = info[...].reshape(chans + 8, 256).astype(jnp.float32)
    masks, names = everyone[:, :CB], everyone[:chans, CB:]
    picked = []
    for d in range(1, R + 1):
        both = masks[:chans] * masks[d : d + chans]
        count = jnp.sum(jnp.where(lanes // 8 == group, both, 0.0), axis=1, keepdims=True)
        factor = 1.0 / (total_segs * jnp.maximum(count, 1.0))
        scale_ref[pl.ds((d - 1) * chans, chans), :] = jnp.broadcast_to(factor, (chans, 256))
        mine = lanes == (d - 1) * G + group
        name = jnp.sum(jnp.where(mine, names, 0.0), axis=1, keepdims=True)
        bin_of = lax.broadcasted_iota(jnp.int32, (chans, 256), 1).astype(jnp.float32)
        picked.append(jnp.where(jnp.broadcast_to(name, (chans, 256)) == bin_of, 1.0, 0.0))
    onehot[...] = jnp.concatenate(picked, 0).T.astype(jnp.bfloat16)

    here(len(STEPS) - 1)

    def hand_over(n, chunk):
        return pltpu.make_async_remote_copy(
            raw.at[chunk],
            raw_in.at[n],
            raw_send.at[n],
            raw_recv.at[n],
            device_id={"seg": other_core},
            device_id_type=MESH,
        )

    def finish_quarter(chunk):
        loop(0, chans // 4, lambda n: products(3, chunk, n * 4))

        def reduce_rows(n):
            at = pl.ds(pl.multiple_of(n * 8, 8), 8)
            raw[chunk, at, :] = acc[chunk, at].sum(1)

        loop(0, tiles // 8, reduce_rows)

    chip = seg - seg % 2
    far = 2 - chip

    def give(n):
        chunk = jnp.where(n == 0, far, chip) + other_core % 2
        finish_quarter(chunk)
        hand_over(n, chunk).start()

    loop(0, 2, give)
    cross_chip = pltpu.make_async_remote_copy(
        half, half_in, half_send, half_recv, device_id={"seg": other_chip}, device_id_type=MESH
    )
    finish_quarter(other_chip)
    hand_over(0, far + other_core % 2).wait()
    half[...] = (raw[other_chip] + raw_in[0]).astype(jnp.bfloat16)
    cross_chip.start()
    finish_quarter(seg)
    hand_over(1, other_core).wait()
    cross_chip.wait()
    sums = raw[seg] + raw_in[1] + half_in[...].astype(jnp.float32)
    sums = sums * scale_ref[...]
    high = sums.astype(jnp.bfloat16)
    low = (sums - high.astype(jnp.float32)).astype(jnp.bfloat16)
    stacked = jnp.dot(onehot[...], high, preferred_element_type=jnp.float32)
    stacked += jnp.dot(onehot[...], low, preferred_element_type=jnp.float32)
    bins[...] = stacked.reshape(chans, BIN_DEV, 256).astype(jnp.bfloat16)

    def deliver(r):
        to = peer(me, r)
        return pltpu.make_async_remote_copy(
            bins.at[to],
            bins_in.at[me],
            bins_send,
            bins_recv,
            device_id={"chan": to},
            device_id_type=MESH,
        )

    for r in range(1, chans):
        deliver(r).start()
    bins_in[me] = bins[me]
    await_all(bins_in, bins_recv)
    halves = []
    for h in range(2):
        total = bins_in[h].astype(jnp.float32)
        for g in range(1, G):
            total = total + bins_in[2 * g + h].astype(jnp.float32)
        halves.append(total)
    spectra = jnp.concatenate(halves, axis=1)
    high = spectra.astype(jnp.bfloat16)
    low = (spectra - high.astype(jnp.float32)).astype(jnp.bfloat16)
    both = jnp.concatenate([high, low], axis=0)

    def share(hop, n, to):
        return pltpu.make_async_remote_copy(
            part.at[hop, n],
            part_in.at[hop, n],
            part_send.at[hop, n],
            part_recv.at[hop, n],
            device_id={"seg": to},
            device_id_type=MESH,
        )

    chunks = range(NLAG // 512)
    for n in chunks:
        at = pl.ds(n * 512, 512)
        value = jnp.dot(both, inv_hi[:, at], preferred_element_type=jnp.float32)
        value = value[:BIN_DEV] + value[BIN_DEV:]
        value += jnp.dot(high, inv_lo[:, at], preferred_element_type=jnp.float32)
        part[0, n] = value
        share(0, n, other_core).start()
    for n in chunks:
        share(0, n, other_core).wait()
        part[1, n] = part[0, n] + part_in[0, n]
        share(1, n, other_chip).start()
    for n in chunks:
        at = pl.ds(n * 512, 512)
        share(1, n, other_chip).wait()
        out_ref[:, at] = part[1, n] + part_in[1, n]

    for i in range(len(STEPS)):
        await_step(send, i, send_sem)
    await_all(info, info_send)
    await_all(bins_in, bins_send)


def per_device(traces, channel_mask, owner_ids, local_bins):
    chans, quarters = lax.axis_size("chan"), lax.axis_size("seg")
    tiles, steps = chans * R, len(STEPS)
    vmem = pl.BlockSpec(memory_space=pltpu.VMEM)
    anywhere = pl.BlockSpec(memory_space=pl.ANY)
    dma = pltpu.SemaphoreType.DMA
    bf16, f32 = jnp.bfloat16, jnp.float32
    return pl.pallas_call(
        functools.partial(stack_kernel, float(traces.shape[0] * quarters)),
        out_shape=jax.ShapeDtypeStruct((BIN_DEV, NLAG), f32),
        in_specs=[anywhere] + [vmem] * 4 + [anywhere] + [vmem] * 4,
        out_specs=vmem,
        scratch_shapes=[
            pltpu.VMEM(traces.shape, bf16),
            pltpu.VMEM((NT, 2 * NB), bf16),
            pltpu.VMEM((2 * CB, 2 * NB), f32),
            pltpu.VMEM((2 * CB, NB + 256), bf16),
            pltpu.VMEM((2 * CB, NB), f32),
            pltpu.VMEM((CB, CB), f32),
            pltpu.VMEM((2, chans, 8, NB), bf16),
            pltpu.VMEM((2, chans + R, 8, NB), bf16),
            pltpu.VMEM((3, chans, 2, 8, NB), bf16),
            pltpu.VMEM((3, chans + R, 2, 8, NB), bf16),
            pltpu.VMEM((4, tiles, 8, 256), f32),
            pltpu.VMEM((1, 2 * CB), jnp.int32),
            pltpu.VMEM((2, 2, 128, 128), f32),
            pltpu.VMEM((512, NLAG), bf16),
            pltpu.VMEM((512, NLAG), bf16),
            pltpu.VMEM((chans + 8, 1, 256), jnp.int32),
            pltpu.VMEM((256, tiles), bf16),
            pltpu.VMEM((tiles, 256), f32),
            pltpu.VMEM((4, tiles, 256), f32),
            pltpu.VMEM((2, tiles, 256), f32),
            pltpu.VMEM((tiles, 256), bf16),
            pltpu.VMEM((tiles, 256), bf16),
            pltpu.VMEM((chans, BIN_DEV, 256), bf16),
            pltpu.VMEM((chans, BIN_DEV, 256), bf16),
            pltpu.VMEM((2, 4, BIN_DEV, NLAG // 4), f32),
            pltpu.VMEM((2, 4, BIN_DEV, NLAG // 4), f32),
            dma((steps,)), dma, dma((steps,)), dma((steps,)), dma((steps,)),
            dma, dma, dma((2,)), dma((2,)), dma, dma, dma, dma, dma((2, 4)), dma((2, 4)),
        ],
        compiler_params=pltpu.CompilerParams(
            collective_id=0, has_side_effects=True, vmem_limit_bytes=60 << 20
        ),
        name="stack",
    )(
        traces,
        *forward_factors(),
        *inverse_factors(),
        channel_mask.reshape(1, -1),
        owner_ids.reshape(1, -1),
        local_bins,
    )


def solution(mesh):
    in_specs = (P("seg", "chan", None), P("chan"), P("chan", None, None), P("chan", None))
    return jax.shard_map(
        per_device, mesh=mesh, in_specs=in_specs, out_specs=P("chan", None), check_vma=False
    )
```

```python
import functools
import math

import jax
import jax.numpy as jnp
import numpy as np
from jax import lax
from jax.experimental import pallas as pl
from jax.experimental.pallas import tpu as pltpu
from jax.sharding import PartitionSpec as P

CB = 128
NT = 4096
K0 = 8
HW = 64
R = 4
G = 16
BIN_DEV = 8
NB = 1024
NLAG = 2048
HALF = NB // 2
QUARTER = NT // 4
EPSILON = 1e-06
STEPS = ((0, 1), (1, 1), (2, 2), (4, 2), (6, 2))
MESH = pl.DeviceIdType.MESH


def forward_factors():
    freqs = K0 + np.arange(NB)
    unit = 2.0 * math.pi / NT
    coarse = (np.arange(16)[:, None, None] * 64 * freqs[None, None, :]) % NT * unit
    fine = (np.arange(64)[:, None] * freqs[None, :]) % NT * unit
    tables = (np.cos(coarse), -np.sin(coarse), np.cos(fine), -np.sin(fine))
    return [jnp.asarray(t, jnp.float32) for t in tables]


def inverse_factors():
    unit = 2.0 * math.pi / NT
    freqs = K0 + np.arange(NB)
    fine = (freqs[:, None] * np.arange(128)[None, :] * 2) % NT * unit
    coarse = (freqs[None, :16] * (np.arange(16)[:, None] * 128 - NLAG // 2) * 2) % NT * unit
    fine = np.stack([np.cos(fine), np.sin(fine)]).reshape(2, 2, 4, 128, 128)
    coarse = np.stack([np.cos(coarse), np.sin(coarse)]) / math.sqrt(NB)
    coarse = np.broadcast_to(coarse[..., None], (2, 16, 16, 128))
    return [jnp.asarray(fine, jnp.float32), jnp.asarray(coarse, jnp.float32)]


def peer(c, r):
    x, y, z = c % 2, (c // 2) % 4, c // 8
    return ((z + r % 4) % 4) * 8 + ((y + (r // 4) % 4) % 4) * 2 + (x + r // 16) % 2


def loop(first, last, body):
    def step(n, carry):
        body(n)
        return carry

    lax.fori_loop(first, last, step, 0)


def stack_kernel(
    total_segs,
    traces, coarse_re, coarse_im, fine_re, fine_im, inv_fine, inv_coarse, mask_row, owners, locals_,
    out_ref,
    x_ref, tab, parts, spec, power, inv_level, valid_ref, send_one, recv_one, send_two, recv_two, acc,
    info_ref, fine_ref, inv_hi, inv_lo, info, onehot, scale_ref, raw, raw_in, half, half_in,
    bins, bins_in, part, part_in,
    x_sem, fine_sem, own_sem, send_sem, recv_sem, info_send, info_recv, raw_send, raw_recv,
    half_send, half_recv, bins_send, bins_recv, part_send, part_recv,
):
    chans = lax.axis_size("chan")
    me = lax.axis_index("chan")
    seg = lax.axis_index("seg")
    other_core = seg + 1 - 2 * (seg % 2)
    other_chip = (seg + 2) % 4
    tiles = chans * R

    def load(i):
        at = pl.ds(*STEPS[i])
        return [
            pltpu.make_async_copy(
                traces.at[at, :, pl.ds(q * QUARTER, QUARTER)], x_ref.at[at, q], x_sem.at[i, q]
            )
            for q in range(4)
        ]

    def load_fine():
        return pltpu.make_async_copy(inv_fine.at[:, :, seg], fine_ref, fine_sem)

    for i in range(len(STEPS)):
        for copy in load(i):
            copy.start()
    load_fine().start()
    info_ref[:, pl.ds(0, CB)] = mask_row[...]
    info_ref[:, pl.ds(CB, CB)] = jnp.zeros((1, CB), jnp.int32)
    info_ref[:, pl.ds(CB, R * G)] = owners[...] * BIN_DEV + locals_[...]

    barrier = pltpu.get_barrier_semaphore()

    def greet(r):
        pl.semaphore_signal(barrier, inc=1, device_id={"chan": peer(me, r)}, device_id_type=MESH)

    for to in (other_core, other_chip):
        pl.semaphore_signal(barrier, inc=1, device_id={"seg": to}, device_id_type=MESH)
    loop(1, chans, greet)

    def make_rows(a):
        at = pl.ds(pl.multiple_of(a * 64, 64), 64)
        for chunk in range(NB // 128):
            cols = pl.ds(chunk * 128, 128)
            ar, ai = coarse_re[a, :, cols], coarse_im[a, :, cols]
            br, bi = fine_re[:, cols], fine_im[:, cols]
            base = (chunk // 4) * NB + (chunk % 4) * 128
            tab[at, pl.ds(base, 128)] = (ar * br - ai * bi).astype(jnp.bfloat16)
            tab[at, pl.ds(base + HALF, 128)] = (ar * bi + ai * br).astype(jnp.bfloat16)

    loop(0, QUARTER // 64, make_rows)

    turn = lax.broadcasted_iota(jnp.int32, (16, 256), 1) % 4
    c0 = jnp.where(turn == 0, 1.0, jnp.where(turn == 2, -1.0, 0.0))
    c1 = jnp.where(turn == 1, 1.0, jnp.where(turn == 3, -1.0, 0.0))
    flip = jnp.where(turn % 2 == 0, 1.0, -1.0)

    own = jnp.broadcast_to(info_ref[:, pl.ds(0, CB)].astype(jnp.float32), (CB, CB))
    diagonal = lax.broadcasted_iota(jnp.int32, (CB, CB), 0) == lax.broadcasted_iota(
        jnp.int32, (CB, CB), 1
    )
    column = jnp.sum(jnp.where(diagonal, own, 0.0), axis=1, keepdims=True)
    valid_ref[...] = jnp.broadcast_to(column, (CB, CB))

    power[:, pl.ds(0, 128)] = jnp.zeros((2 * CB, 128), jnp.bfloat16)
    power[:, pl.ds(128 + NB, 128)] = jnp.zeros((2 * CB, 128), jnp.bfloat16)
    near = (
        lax.broadcasted_iota(jnp.int32, (512, 256), 0)
        - lax.broadcasted_iota(jnp.int32, (512, 256), 1)
        - 128
    )
    band = jnp.where(jnp.abs(near) <= HW, 1.0, 0.0).astype(jnp.bfloat16)

    send = [send_one.at[0], send_one.at[1]] + [send_two.at[i] for i in range(3)]
    recv = [recv_one.at[0], recv_one.at[1]] + [recv_two.at[i] for i in range(3)]

    def exchange(i, r):
        to = peer(me, r)
        return pltpu.make_async_remote_copy(
            send[i].at[to],
            recv[i].at[me],
            send_sem.at[i],
            recv_sem.at[i],
            device_id={"chan": to},
            device_id_type=MESH,
        )

    def keep(i):
        return pltpu.make_async_copy(send[i].at[me], recv[i].at[me], own_sem.at[i])

    def await_all(ref, sem):
        pieces = ref.at[pl.ds(0, chans - 1)]
        pltpu.make_async_copy(pieces, pieces, sem).wait()

    def tell(r):
        to = peer(me, r)
        return pltpu.make_async_remote_copy(
            info_ref,
            info.at[me],
            info_send,
            info_recv,
            device_id={"chan": to},
            device_id_type=MESH,
        )

    def await_step(ref, i, sem):
        pieces = ref[i].at[pl.ds(0, chans - 1)]
        pltpu.make_async_copy(pieces, pieces, sem.at[i]).wait()

    def whiten_step(i):
        first, segs = STEPS[i]
        rows = segs * CB
        every = pl.ds(0, rows)
        for copy in load(i):
            copy.wait()

        def transform(n):
            cols = pl.ds(pl.multiple_of(n * 512, 512), 512)
            block = x_ref[pl.ds(first, segs)].reshape(4 * rows, QUARTER)
            parts[pl.ds(0, 4 * rows), cols] = jnp.dot(
                block, tab[:, cols], preferred_element_type=jnp.float32
            )

        loop(0, 2 * NB // 512, transform)

        def add_power(n):
            at = pl.ds(pl.multiple_of(n * 16, 16), 16)
            s, row = n // (CB // 16), n % (CB // 16)
            for chunk in range(NB // 256):
                base = (chunk // 2) * NB + (chunk % 2) * 256
                res, ims = [], []
                for q in range(4):
                    rows_of = pl.ds(pl.multiple_of((s * 4 + q) * CB + row * 16, 16), 16)
                    res.append(parts[rows_of, pl.ds(base, 256)])
                    ims.append(parts[rows_of, pl.ds(base + HALF, 256)])
                b_re, b_im = res[1] + flip * res[3], ims[1] + flip * ims[3]
                re = res[0] + flip * res[2] + (c0 * b_re + c1 * b_im)
                im = ims[0] + flip * ims[2] + (c0 * b_im - c1 * b_re)
                spec[at, pl.ds(base, 256)] = re
                spec[at, pl.ds(base + HALF, 256)] = im
                power[at, pl.ds(128 + chunk * 256, 256)] = (re * re + im * im).astype(jnp.bfloat16)

        loop(0, rows // 16, add_power)

        for chunk in range(NB // 256):
            total = jnp.dot(
                power[every, pl.ds(chunk * 256, 512)], band, preferred_element_type=jnp.float32
            )
            k = chunk * 256 + lax.broadcasted_iota(jnp.int32, (1, 256), 1)
            count = jnp.minimum(k + HW, NB - 1) - jnp.maximum(k - HW, 0) + 1
            inv_level[every, pl.ds(chunk * 256, 256)] = lax.rsqrt(
                total * (1.0 / count.astype(jnp.float32)) + EPSILON
            )

        def scale(g):
            valid = valid_ref[pl.ds(pl.multiple_of(g * 8, 8), 8), :]
            for s in range(segs):
                row = pl.ds(pl.multiple_of(s * CB + g * 8, 8), 8)
                for chunk in range(NB // 128):
                    h, at = chunk // 4, (chunk % 4) * 128
                    weight = inv_level[row, pl.ds(chunk * 128, 128)] * valid
                    re = spec[row, pl.ds(h * NB + at, 128)] * weight
                    im = spec[row, pl.ds(h * NB + HALF + at, 128)] * weight
                    to = 2 * g + h
                    block = send[i].at[to, s] if segs == 2 else send[i].at[to]
                    block[:, pl.ds(at, 128)] = re.astype(jnp.bfloat16)
                    block[:, pl.ds(HALF + at, 128)] = im.astype(jnp.bfloat16)

        loop(0, G, scale)
        keep(i).start()

    def send_step(i):
        loop(1, chans, lambda r: exchange(i, chans - r).start())

    whiten_step(0)
    pl.semaphore_wait(barrier, chans + 1)
    send_step(0)
    for i in range(1, len(STEPS)):
        whiten_step(i)
        send_step(i)
        if i == 2:
            loop(1, chans, lambda r: tell(r).start())

    for block in recv:
        block[pl.ds(chans, R)] = jnp.zeros((R,) + block.shape[1:], jnp.bfloat16)
    load_fine().wait()

    def make_inverse(n):
        h, at = n // 8, pl.multiple_of((n % 8) * 16, 16)
        br, bi = fine_ref[0, h, pl.ds(at, 16)], fine_ref[1, h, pl.ds(at, 16)]
        for a in range(16):
            ar, ai = inv_coarse[0, a], inv_coarse[1, a]
            re, im = ar * br - ai * bi, -(ar * bi + ai * br)
            for which, value in enumerate((re, im)):
                at_row = pl.ds(pl.multiple_of(h * 256 + which * 128 + at, 16), 16)
                high = value.astype(jnp.bfloat16)
                inv_hi[at_row, pl.ds(a * 128, 128)] = high
                low = value - high.astype(jnp.float32)
                inv_lo[at_row, pl.ds(a * 128, 128)] = low.astype(jnp.bfloat16)

    loop(0, 16, make_inverse)

    def products(pair, chunk, first, add=True):
        re_at = pl.ds(pl.multiple_of(chunk * 128, 128), 128)
        im_at = pl.ds(pl.multiple_of(HALF + chunk * 128, 128), 128)

        def part_of(j, s, at):
            block = recv[s].at[first + j] if pair == 0 else recv[pair + 1].at[first + j, s]
            return block[:, at].astype(jnp.float32)

        re = [[part_of(j, s, re_at) for j in range(4 + R)] for s in range(2)]
        im = [[part_of(j, s, im_at) for j in range(4 + R)] for s in range(2)]
        for j in range(4):
            for d in range(1, R + 1):
                t = (d - 1) * chans + first + j
                p = re[0][j] * re[0][j + d] + im[0][j] * im[0][j + d]
                q = im[0][j] * re[0][j + d] - re[0][j] * im[0][j + d]
                p += re[1][j] * re[1][j + d] + im[1][j] * im[1][j + d]
                q += im[1][j] * re[1][j + d] - re[1][j] * im[1][j + d]
                if add:
                    p = p + acc[chunk, t, :, pl.ds(0, 128)]
                    q = q + acc[chunk, t, :, pl.ds(128, 128)]
                acc[chunk, t, :, pl.ds(0, 128)] = p
                acc[chunk, t, :, pl.ds(128, 128)] = q

    def here(i):
        await_step(recv, i, recv_sem)
        keep(i).wait()

    here(0)
    here(1)
    loop(0, chans, lambda n: products(0, n % 4, (n // 4) * 4, add=False))
    for i in (2, 3):
        here(i)
        loop(0, chans, lambda n: products(i - 1, n % 4, (n // 4) * 4))

    info[pl.ds(me, 1)] = info_ref[...].reshape(1, 1, 256)
    info[pl.ds(chans, 8)] = jnp.zeros((8, 1, 256), jnp.int32)
    await_all(info, info_recv)
    group = me // 2
    lanes = lax.broadcasted_iota(jnp.int32, (chans, CB), 1)
    everyone = info[...].reshape(chans + 8, 256).astype(jnp.float32)
    masks, names = everyone[:, :CB], everyone[:chans, CB:]
    picked = []
    for d in range(1, R + 1):
        both = masks[:chans] * masks[d : d + chans]
        count = jnp.sum(jnp.where(lanes // 8 == group, both, 0.0), axis=1, keepdims=True)
        factor = 1.0 / (total_segs * jnp.maximum(count, 1.0))
        scale_ref[pl.ds((d - 1) * chans, chans), :] = jnp.broadcast_to(factor, (chans, 256))
        mine = lanes == (d - 1) * G + group
        name = jnp.sum(jnp.where(mine, names, 0.0), axis=1, keepdims=True)
        bin_of = lax.broadcasted_iota(jnp.int32, (chans, 256), 1).astype(jnp.float32)
        picked.append(jnp.where(jnp.broadcast_to(name, (chans, 256)) == bin_of, 1.0, 0.0))
    onehot[...] = jnp.concatenate(picked, 0).T.astype(jnp.bfloat16)

    here(len(STEPS) - 1)

    def hand_over(n, chunk):
        return pltpu.make_async_remote_copy(
            raw.at[chunk],
            raw_in.at[n],
            raw_send.at[n],
            raw_recv.at[n],
            device_id={"seg": other_core},
            device_id_type=MESH,
        )

    def finish_quarter(chunk):
        loop(0, chans // 4, lambda n: products(3, chunk, n * 4))

        def reduce_rows(n):
            at = pl.ds(pl.multiple_of(n * 8, 8), 8)
            raw[chunk, at, :] = acc[chunk, at].sum(1)

        loop(0, tiles // 8, reduce_rows)

    chip = seg - seg % 2
    far = 2 - chip

    def give(n):
        chunk = jnp.where(n == 0, far, chip) + other_core % 2
        finish_quarter(chunk)
        hand_over(n, chunk).start()

    loop(0, 2, give)
    cross_chip = pltpu.make_async_remote_copy(
        half, half_in, half_send, half_recv, device_id={"seg": other_chip}, device_id_type=MESH
    )
    finish_quarter(other_chip)
    hand_over(0, far + other_core % 2).wait()
    half[...] = (raw[other_chip] + raw_in[0]).astype(jnp.bfloat16)
    cross_chip.start()
    finish_quarter(seg)
    hand_over(1, other_core).wait()
    cross_chip.wait()
    sums = raw[seg] + raw_in[1] + half_in[...].astype(jnp.float32)
    sums = sums * scale_ref[...]
    high = sums.astype(jnp.bfloat16)
    low = (sums - high.astype(jnp.float32)).astype(jnp.bfloat16)
    stacked = jnp.dot(onehot[...], high, preferred_element_type=jnp.float32)
    stacked += jnp.dot(onehot[...], low, preferred_element_type=jnp.float32)
    bins[...] = stacked.reshape(chans, BIN_DEV, 256).astype(jnp.bfloat16)

    def deliver(r):
        to = peer(me, r)
        return pltpu.make_async_remote_copy(
            bins.at[to],
            bins_in.at[me],
            bins_send,
            bins_recv,
            device_id={"chan": to},
            device_id_type=MESH,
        )

    for r in range(1, chans):
        deliver(r).start()
    bins_in[me] = bins[me]
    await_all(bins_in, bins_recv)
    halves = []
    for h in range(2):
        total = bins_in[h].astype(jnp.float32)
        for g in range(1, G):
            total = total + bins_in[2 * g + h].astype(jnp.float32)
        halves.append(total)
    spectra = jnp.concatenate(halves, axis=1)
    high = spectra.astype(jnp.bfloat16)
    low = (spectra - high.astype(jnp.float32)).astype(jnp.bfloat16)
    both = jnp.concatenate([high, low], axis=0)

    def share(n, q):
        return pltpu.make_async_remote_copy(
            part.at[n],
            part_in.at[n, seg],
            part_send.at[n, q],
            part_recv.at[n, seg],
            device_id={"seg": (seg + q) % 4},
            device_id_type=MESH,
        )

    width = NLAG // 2
    for n in range(2):
        at = pl.ds(n * width, width)
        value = jnp.dot(both, inv_hi[:, at], preferred_element_type=jnp.float32)
        value = value[:BIN_DEV] + value[BIN_DEV:]
        value += jnp.dot(high, inv_lo[:, at], preferred_element_type=jnp.float32)
        part[n] = value.astype(jnp.bfloat16)
        for q in (2, 1, 3):
            share(n, q).start()
        part_in[n, seg] = value.astype(jnp.bfloat16)
    for n in range(2):
        for q in (1, 2, 3):
            source = part_in.at[n, (seg + q) % 4]
            pltpu.make_async_copy(source, source, part_recv.at[n, (seg + q) % 4]).wait()
        terms = [part_in[n, q].astype(jnp.float32) for q in range(4)]
        out_ref[:, pl.ds(n * width, width)] = (terms[0] + terms[1]) + (terms[2] + terms[3])

    for n in range(2):
        for q in (1, 2, 3):
            share(n, q).wait_send()
    for i in range(len(STEPS)):
        await_step(send, i, send_sem)
    await_all(info, info_send)
    await_all(bins_in, bins_send)


def per_device(traces, channel_mask, owner_ids, local_bins):
    chans, quarters = lax.axis_size("chan"), lax.axis_size("seg")
    tiles, steps = chans * R, len(STEPS)
    vmem = pl.BlockSpec(memory_space=pltpu.VMEM)
    anywhere = pl.BlockSpec(memory_space=pl.ANY)
    dma = pltpu.SemaphoreType.DMA
    bf16, f32 = jnp.bfloat16, jnp.float32
    return pl.pallas_call(
        functools.partial(stack_kernel, float(traces.shape[0] * quarters)),
        out_shape=jax.ShapeDtypeStruct((BIN_DEV, NLAG), f32),
        in_specs=[anywhere] + [vmem] * 4 + [anywhere] + [vmem] * 4,
        out_specs=vmem,
        scratch_shapes=[
            pltpu.VMEM((traces.shape[0], 4, CB, QUARTER), bf16),
            pltpu.VMEM((QUARTER, 2 * NB), bf16),
            pltpu.VMEM((8 * CB, 2 * NB), f32),
            pltpu.VMEM((2 * CB, 2 * NB), f32),
            pltpu.VMEM((2 * CB, NB + 256), bf16),
            pltpu.VMEM((2 * CB, NB), f32),
            pltpu.VMEM((CB, CB), f32),
            pltpu.VMEM((2, chans, 8, NB), bf16),
            pltpu.VMEM((2, chans + R, 8, NB), bf16),
            pltpu.VMEM((3, chans, 2, 8, NB), bf16),
            pltpu.VMEM((3, chans + R, 2, 8, NB), bf16),
            pltpu.VMEM((4, tiles, 8, 256), f32),
            pltpu.VMEM((1, 2 * CB), jnp.int32),
            pltpu.VMEM((2, 2, 128, 128), f32),
            pltpu.VMEM((512, NLAG), bf16),
            pltpu.VMEM((512, NLAG), bf16),
            pltpu.VMEM((chans + 8, 1, 256), jnp.int32),
            pltpu.VMEM((256, tiles), bf16),
            pltpu.VMEM((tiles, 256), f32),
            pltpu.VMEM((4, tiles, 256), f32),
            pltpu.VMEM((2, tiles, 256), f32),
            pltpu.VMEM((tiles, 256), bf16),
            pltpu.VMEM((tiles, 256), bf16),
            pltpu.VMEM((chans, BIN_DEV, 256), bf16),
            pltpu.VMEM((chans, BIN_DEV, 256), bf16),
            pltpu.VMEM((2, BIN_DEV, NLAG // 2), bf16),
            pltpu.VMEM((2, 4, BIN_DEV, NLAG // 2), bf16),
            dma((steps, 4)), dma, dma((steps,)), dma((steps,)), dma((steps,)),
            dma, dma, dma((2,)), dma((2,)), dma, dma, dma, dma, dma((2, 4)), dma((2, 4)),
        ],
        compiler_params=pltpu.CompilerParams(
            collective_id=0, has_side_effects=True, vmem_limit_bytes=60 << 20
        ),
        name="stack",
    )(
        traces,
        *forward_factors(),
        *inverse_factors(),
        channel_mask.reshape(1, -1),
        owner_ids.reshape(1, -1),
        local_bins,
    )


def solution(mesh):
    in_specs = (P("seg", "chan", None), P("chan"), P("chan", None, None), P("chan", None))
    return jax.shard_map(
        per_device, mesh=mesh, in_specs=in_specs, out_specs=P("chan", None), check_vma=False
    )
```

```python
import functools
import math

import jax
import jax.numpy as jnp
import numpy as np
from jax import lax
from jax.experimental import pallas as pl
from jax.experimental.pallas import tpu as pltpu
from jax.sharding import PartitionSpec as P

CB = 128
NT = 4096
K0 = 8
HW = 64
R = 4
G = 16
BIN_DEV = 8
NB = 1024
NLAG = 2048
HALF = NB // 2
QUARTER = NT // 4
EPSILON = 1e-06
STEPS = ((0, 1), (1, 1), (2, 2), (4, 2), (6, 1), (7, 1))
MESH = pl.DeviceIdType.MESH


def forward_factors():
    freqs = K0 + np.arange(NB)
    unit = 2.0 * math.pi / NT
    coarse = (np.arange(16)[:, None, None] * 64 * freqs[None, None, :]) % NT * unit
    fine = (np.arange(64)[:, None] * freqs[None, :]) % NT * unit
    tables = (np.cos(coarse), -np.sin(coarse), np.cos(fine), -np.sin(fine))
    return [jnp.asarray(t, jnp.float32) for t in tables]


def inverse_factors():
    unit = 2.0 * math.pi / NT
    freqs = K0 + np.arange(NB)
    fine = (freqs[:, None] * np.arange(128)[None, :] * 2) % NT * unit
    coarse = (freqs[None, :16] * (np.arange(16)[:, None] * 128 - NLAG // 2) * 2) % NT * unit
    fine = np.stack([np.cos(fine), np.sin(fine)]).reshape(2, 2, 4, 128, 128)
    coarse = np.stack([np.cos(coarse), np.sin(coarse)]) / math.sqrt(NB)
    coarse = np.broadcast_to(coarse[..., None], (2, 16, 16, 128))
    return [jnp.asarray(fine, jnp.float32), jnp.asarray(coarse, jnp.float32)]


def peer(c, r):
    x, y, z = c % 2, (c // 2) % 4, c // 8
    return ((z + r % 4) % 4) * 8 + ((y + (r // 4) % 4) % 4) * 2 + (x + r // 16) % 2


def loop(first, last, body):
    def step(n, carry):
        body(n)
        return carry

    lax.fori_loop(first, last, step, 0)


def stack_kernel(
    total_segs,
    traces, coarse_re, coarse_im, fine_re, fine_im, inv_fine, inv_coarse_hbm, mask_row, owners, locals_,
    out_ref,
    x_ref, tab, parts, spec, power, inv_level, valid_ref, send_one, recv_one, send_two, recv_two, acc,
    info_ref, fine_ref, inv_coarse, inv_hi, inv_lo, info, onehot, scale_ref, raw, raw_in, bins, bins_in, part, part_in,
    x_sem, fine_sem, own_sem, send_sem, recv_sem, info_send, info_recv, raw_send, raw_recv,
    bins_send, bins_recv, part_send, part_recv, entered,
):
    chans = lax.axis_size("chan")
    me = lax.axis_index("chan")
    seg = lax.axis_index("seg")
    other_core = seg + 1 - 2 * (seg % 2)
    other_chip = (seg + 2) % 4
    tiles = chans * R

    def load(i):
        at = pl.ds(*STEPS[i])
        return [
            pltpu.make_async_copy(
                traces.at[at, :, pl.ds(q * QUARTER, QUARTER)], x_ref.at[at, q], x_sem.at[i, q]
            )
            for q in range(4)
        ]

    def load_fine():
        return (
            pltpu.make_async_copy(inv_fine.at[:, :, seg], fine_ref, fine_sem.at[0]),
            pltpu.make_async_copy(inv_coarse_hbm, inv_coarse, fine_sem.at[1]),
        )

    for i in range(len(STEPS)):
        for copy in load(i):
            copy.start()
    for copy in load_fine():
        copy.start()
    info_ref[:, pl.ds(0, CB)] = mask_row[...]
    info_ref[:, pl.ds(CB, CB)] = jnp.zeros((1, CB), jnp.int32)
    info_ref[:, pl.ds(CB, R * G)] = owners[...] * BIN_DEV + locals_[...]

    barrier = pltpu.get_barrier_semaphore()

    def greet(r):
        pl.semaphore_signal(barrier, inc=1, device_id={"chan": peer(me, r)}, device_id_type=MESH)

    for to in (other_core, other_chip):
        pl.semaphore_signal(barrier, inc=1, device_id={"seg": to}, device_id_type=MESH)

    def make_rows(a):
        greet(2 * a + 1)
        at = pl.ds(pl.multiple_of(a * 64, 64), 64)
        for chunk in range(NB // 128):
            cols = pl.ds(chunk * 128, 128)
            ar, ai = coarse_re[a, :, cols], coarse_im[a, :, cols]
            br, bi = fine_re[:, cols], fine_im[:, cols]
            base = (chunk // 4) * NB + (chunk % 4) * 128
            tab[at, pl.ds(base, 128)] = (ar * br - ai * bi).astype(jnp.bfloat16)
            tab[at, pl.ds(base + HALF, 128)] = (ar * bi + ai * br).astype(jnp.bfloat16)

    def make_rows_and_greet(a):
        greet(2 * a + 2)
        make_rows(a)

    loop(0, chans // 2 - 1, make_rows_and_greet)
    make_rows(chans // 2 - 1)

    turn = lax.broadcasted_iota(jnp.int32, (16, 256), 1) % 4
    c0 = jnp.where(turn == 0, 1.0, jnp.where(turn == 2, -1.0, 0.0))
    c1 = jnp.where(turn == 1, 1.0, jnp.where(turn == 3, -1.0, 0.0))
    flip = jnp.where(turn % 2 == 0, 1.0, -1.0)

    own = jnp.broadcast_to(info_ref[:, pl.ds(0, CB)].astype(jnp.float32), (CB, CB))
    diagonal = lax.broadcasted_iota(jnp.int32, (CB, CB), 0) == lax.broadcasted_iota(
        jnp.int32, (CB, CB), 1
    )
    column = jnp.sum(jnp.where(diagonal, own, 0.0), axis=1, keepdims=True)
    valid_ref[...] = jnp.broadcast_to(column, (CB, CB))

    power[:, pl.ds(0, 128)] = jnp.zeros((2 * CB, 128), jnp.bfloat16)
    power[:, pl.ds(128 + NB, 128)] = jnp.zeros((2 * CB, 128), jnp.bfloat16)
    near = (
        lax.broadcasted_iota(jnp.int32, (512, 256), 0)
        - lax.broadcasted_iota(jnp.int32, (512, 256), 1)
        - 128
    )
    band = jnp.where(jnp.abs(near) <= HW, 1.0, 0.0).astype(jnp.bfloat16)

    send = [send_one.at[0], send_one.at[1], send_two.at[0], send_two.at[1], send_one.at[2], send_one.at[3]]
    recv = [recv_one.at[0], recv_one.at[1], recv_two.at[0], recv_two.at[1], recv_one.at[2], recv_one.at[3]]

    def exchange(i, r):
        to = peer(me, r)
        return pltpu.make_async_remote_copy(
            send[i].at[to],
            recv[i].at[me],
            send_sem.at[i],
            recv_sem.at[i],
            device_id={"chan": to},
            device_id_type=MESH,
        )

    def keep(i):
        return pltpu.make_async_copy(send[i].at[me], recv[i].at[me], own_sem.at[i])

    def await_all(ref, sem):
        pieces = ref.at[pl.ds(0, chans - 1)]
        pltpu.make_async_copy(pieces, pieces, sem).wait()

    def tell(r):
        to = peer(me, r)
        return pltpu.make_async_remote_copy(
            info_ref,
            info.at[me],
            info_send,
            info_recv,
            device_id={"chan": to},
            device_id_type=MESH,
        )

    def await_step(ref, i, sem):
        pieces = ref[i].at[pl.ds(0, chans - 1)]
        pltpu.make_async_copy(pieces, pieces, sem.at[i]).wait()

    def whiten_step(i):
        first, segs = STEPS[i]
        rows = segs * CB
        every = pl.ds(0, rows)
        for copy in load(i):
            copy.wait()

        def transform(n):
            cols = pl.ds(pl.multiple_of(n * 512, 512), 512)
            block = x_ref[pl.ds(first, segs)].reshape(4 * rows, QUARTER)
            parts[pl.ds(0, 4 * rows), cols] = jnp.dot(
                block, tab[:, cols], preferred_element_type=jnp.float32
            )

        loop(0, 2 * NB // 512, transform)

        def add_power(n):
            at = pl.ds(pl.multiple_of(n * 16, 16), 16)
            s, row = n // (CB // 16), n % (CB // 16)
            for chunk in range(NB // 256):
                base = (chunk // 2) * NB + (chunk % 2) * 256
                res, ims = [], []
                for q in range(4):
                    rows_of = pl.ds(pl.multiple_of((s * 4 + q) * CB + row * 16, 16), 16)
                    res.append(parts[rows_of, pl.ds(base, 256)])
                    ims.append(parts[rows_of, pl.ds(base + HALF, 256)])
                b_re, b_im = res[1] + flip * res[3], ims[1] + flip * ims[3]
                re = res[0] + flip * res[2] + (c0 * b_re + c1 * b_im)
                im = ims[0] + flip * ims[2] + (c0 * b_im - c1 * b_re)
                spec[at, pl.ds(base, 256)] = re
                spec[at, pl.ds(base + HALF, 256)] = im
                power[at, pl.ds(128 + chunk * 256, 256)] = (re * re + im * im).astype(jnp.bfloat16)

        loop(0, rows // 16, add_power)

        for chunk in range(NB // 256):
            total = jnp.dot(
                power[every, pl.ds(chunk * 256, 512)], band, preferred_element_type=jnp.float32
            )
            k = chunk * 256 + lax.broadcasted_iota(jnp.int32, (1, 256), 1)
            count = jnp.minimum(k + HW, NB - 1) - jnp.maximum(k - HW, 0) + 1
            inv_level[every, pl.ds(chunk * 256, 256)] = lax.rsqrt(
                total * (1.0 / count.astype(jnp.float32)) + EPSILON
            )

        def scale(g):
            valid = valid_ref[pl.ds(pl.multiple_of(g * 8, 8), 8), :]
            for s in range(segs):
                row = pl.ds(pl.multiple_of(s * CB + g * 8, 8), 8)
                for chunk in range(NB // 128):
                    h, at = chunk // 4, (chunk % 4) * 128
                    weight = inv_level[row, pl.ds(chunk * 128, 128)] * valid
                    re = spec[row, pl.ds(h * NB + at, 128)] * weight
                    im = spec[row, pl.ds(h * NB + HALF + at, 128)] * weight
                    to = 2 * g + h
                    block = send[i].at[to, s] if segs == 2 else send[i].at[to]
                    block[:, pl.ds(at, 128)] = re.astype(jnp.bfloat16)
                    block[:, pl.ds(HALF + at, 128)] = im.astype(jnp.bfloat16)

        loop(0, G, scale)
        keep(i).start()

    def send_step(i):
        loop(1, chans, lambda r: exchange(i, chans - r).start())

    whiten_step(0)
    pl.semaphore_wait(barrier, chans + 1)
    pl.semaphore_signal(entered, inc=1, device_id={"seg": other_chip}, device_id_type=MESH)
    send_step(0)
    for i in range(1, len(STEPS)):
        whiten_step(i)
        send_step(i)
        if i == 2:
            loop(1, chans, lambda r: tell(r).start())

    for block in recv:
        block[pl.ds(chans, R)] = jnp.zeros((R,) + block.shape[1:], jnp.bfloat16)
    for copy in load_fine():
        copy.wait()

    def make_inverse(n):
        h, at = n // 8, pl.multiple_of((n % 8) * 16, 16)
        br, bi = fine_ref[0, h, pl.ds(at, 16)], fine_ref[1, h, pl.ds(at, 16)]
        for a in range(16):
            ar, ai = inv_coarse[0, a], inv_coarse[1, a]
            re, im = ar * br - ai * bi, -(ar * bi + ai * br)
            for which, value in enumerate((re, im)):
                at_row = pl.ds(pl.multiple_of(h * 256 + which * 128 + at, 16), 16)
                high = value.astype(jnp.bfloat16)
                inv_hi[at_row, pl.ds(a * 128, 128)] = high
                low = value - high.astype(jnp.float32)
                inv_lo[at_row, pl.ds(a * 128, 128)] = low.astype(jnp.bfloat16)

    loop(0, 16, make_inverse)

    def products(steps, chunk, first, add=True):
        re_at = pl.ds(pl.multiple_of(chunk * 128, 128), 128)
        im_at = pl.ds(pl.multiple_of(HALF + chunk * 128, 128), 128)
        blocks = []
        for i in steps:
            two = STEPS[i][1] == 2
            for s in range(STEPS[i][1]):
                blocks.append(
                    [recv[i].at[first + j, s] if two else recv[i].at[first + j] for j in range(4 + R)]
                )
        re = [[ref[:, re_at].astype(jnp.float32) for ref in refs] for refs in blocks]
        im = [[ref[:, im_at].astype(jnp.float32) for ref in refs] for refs in blocks]
        for j in range(4):
            for d in range(1, R + 1):
                t = (d - 1) * chans + first + j
                p, q = (0.0, 0.0) if not add else (
                    acc[chunk, t, :, pl.ds(0, 128)], acc[chunk, t, :, pl.ds(128, 128)]
                )
                for s in range(len(blocks)):
                    p = p + (re[s][j] * re[s][j + d] + im[s][j] * im[s][j + d])
                    q = q + (im[s][j] * re[s][j + d] - re[s][j] * im[s][j + d])
                acc[chunk, t, :, pl.ds(0, 128)] = p
                acc[chunk, t, :, pl.ds(128, 128)] = q

    def here(i):
        await_step(recv, i, recv_sem)
        keep(i).wait()

    here(0)
    here(1)
    loop(0, chans, lambda n: products((0, 1), n % 4, (n // 4) * 4, add=False))
    for i in (2, 3, 4):
        here(i)
        loop(0, chans, lambda n: products((i,), n % 4, (n // 4) * 4))

    info[pl.ds(me, 1)] = info_ref[...].reshape(1, 1, 256)
    info[pl.ds(chans, 8)] = jnp.zeros((8, 1, 256), jnp.int32)
    await_all(info, info_recv)
    group = me // 2
    lanes = lax.broadcasted_iota(jnp.int32, (chans, CB), 1)
    everyone = info[...].reshape(chans + 8, 256).astype(jnp.float32)
    masks, names = everyone[:, :CB], everyone[:chans, CB:]
    picked = []
    for d in range(1, R + 1):
        both = masks[:chans] * masks[d : d + chans]
        count = jnp.sum(jnp.where(lanes // 8 == group, both, 0.0), axis=1, keepdims=True)
        factor = 1.0 / (total_segs * jnp.maximum(count, 1.0))
        scale_ref[pl.ds((d - 1) * chans, chans), :] = jnp.broadcast_to(factor, (chans, 256))
        mine = lanes == (d - 1) * G + group
        name = jnp.sum(jnp.where(mine, names, 0.0), axis=1, keepdims=True)
        bin_of = lax.broadcasted_iota(jnp.int32, (chans, 256), 1).astype(jnp.float32)
        picked.append(jnp.where(jnp.broadcast_to(name, (chans, 256)) == bin_of, 1.0, 0.0))
    onehot[...] = jnp.concatenate(picked, 0).T.astype(jnp.bfloat16)

    here(len(STEPS) - 1)

    def hand_over(n, chunk):
        return pltpu.make_async_remote_copy(
            raw.at[chunk],
            raw_in.at[n],
            raw_send.at[n],
            raw_recv.at[n],
            device_id={"seg": other_core},
            device_id_type=MESH,
        )

    def finish_quarter(chunk):
        loop(0, chans // 4, lambda n: products((len(STEPS) - 1,), chunk, n * 4))

        def reduce_rows(n):
            at = pl.ds(pl.multiple_of(n * 8, 8), 8)
            raw[chunk, at, :] = acc[chunk, at].sum(1)

        loop(0, tiles // 8, reduce_rows)

    chip = seg - seg % 2
    far = 2 - chip

    def give(n, chunk):
        finish_quarter(chunk)
        hand_over(n, chunk).start()

    def stack(n, sums):
        sums = sums * scale_ref[...]
        high = sums.astype(jnp.bfloat16)
        low = (sums - high.astype(jnp.float32)).astype(jnp.bfloat16)
        stacked = jnp.dot(onehot[...], high, preferred_element_type=jnp.float32)
        stacked += jnp.dot(onehot[...], low, preferred_element_type=jnp.float32)
        bins[n] = stacked.reshape(chans, BIN_DEV, 256).astype(jnp.bfloat16)

    def deliver(n, r):
        to = peer(me, r)
        return pltpu.make_async_remote_copy(
            bins.at[n, to],
            bins_in.at[n * chans + me],
            bins_send,
            bins_recv,
            device_id={"seg": other_chip if n else seg, "chan": to},
            device_id_type=MESH,
        )

    give(0, far + other_core % 2)
    finish_quarter(other_chip)
    give(1, other_core)
    hand_over(0, far + other_core % 2).wait()
    stack(1, raw[other_chip] + raw_in[0])
    pl.semaphore_wait(entered, 1)
    loop(0, chans, lambda r: deliver(1, chans - 1 - r).start())
    finish_quarter(seg)
    hand_over(1, other_core).wait()
    stack(0, raw[seg] + raw_in[1])
    loop(1, chans, lambda r: deliver(0, chans - r).start())
    bins_in[me] = bins[0, me]
    pieces = bins_in.at[pl.ds(0, 2 * chans - 1)]
    pltpu.make_async_copy(pieces, pieces, bins_recv).wait()
    halves = []
    for h in range(2):
        total = bins_in[h].astype(jnp.float32)
        for g in range(1, 2 * G):
            total = total + bins_in[2 * g + h].astype(jnp.float32)
        halves.append(total)
    spectra = jnp.concatenate(halves, axis=1)
    high = spectra.astype(jnp.bfloat16)
    low = (spectra - high.astype(jnp.float32)).astype(jnp.bfloat16)
    both = jnp.concatenate([high, low], axis=0)

    def share(n, q):
        return pltpu.make_async_remote_copy(
            part.at[n],
            part_in.at[n, seg],
            part_send.at[n, q],
            part_recv.at[n, seg],
            device_id={"seg": (seg + q) % 4},
            device_id_type=MESH,
        )

    width = NLAG // 2
    for n in range(2):
        at = pl.ds(n * width, width)
        value = jnp.dot(both, inv_hi[:, at], preferred_element_type=jnp.float32)
        value = value[:BIN_DEV] + value[BIN_DEV:]
        value += jnp.dot(high, inv_lo[:, at], preferred_element_type=jnp.float32)
        part[n] = value.astype(jnp.bfloat16)
        for q in (2, 1, 3):
            share(n, q).start()
        part_in[n, seg] = value.astype(jnp.bfloat16)
    for n in range(2):
        for q in (1, 2, 3):
            source = part_in.at[n, (seg + q) % 4]
            pltpu.make_async_copy(source, source, part_recv.at[n, (seg + q) % 4]).wait()
        terms = [part_in[n, q].astype(jnp.float32) for q in range(4)]
        out_ref[:, pl.ds(n * width, width)] = (terms[0] + terms[1]) + (terms[2] + terms[3])

    for n in range(2):
        for q in (1, 2, 3):
            share(n, q).wait_send()
    for i in range(len(STEPS)):
        await_step(send, i, send_sem)
    await_all(info, info_send)
    pltpu.make_async_copy(pieces, pieces, bins_send).wait()


def per_device(traces, channel_mask, owner_ids, local_bins):
    chans, quarters = lax.axis_size("chan"), lax.axis_size("seg")
    tiles, steps = chans * R, len(STEPS)
    vmem = pl.BlockSpec(memory_space=pltpu.VMEM)
    anywhere = pl.BlockSpec(memory_space=pl.ANY)
    dma = pltpu.SemaphoreType.DMA
    bf16, f32 = jnp.bfloat16, jnp.float32
    return pl.pallas_call(
        functools.partial(stack_kernel, float(traces.shape[0] * quarters)),
        out_shape=jax.ShapeDtypeStruct((BIN_DEV, NLAG), f32),
        in_specs=[anywhere] + [vmem] * 4 + [anywhere] * 2 + [vmem] * 3,
        out_specs=vmem,
        scratch_shapes=[
            pltpu.VMEM((traces.shape[0], 4, CB, QUARTER), bf16),
            pltpu.VMEM((QUARTER, 2 * NB), bf16),
            pltpu.VMEM((8 * CB, 2 * NB), f32),
            pltpu.VMEM((2 * CB, 2 * NB), f32),
            pltpu.VMEM((2 * CB, NB + 256), bf16),
            pltpu.VMEM((2 * CB, NB), f32),
            pltpu.VMEM((CB, CB), f32),
            pltpu.VMEM((4, chans, 8, NB), bf16),
            pltpu.VMEM((4, chans + R, 8, NB), bf16),
            pltpu.VMEM((2, chans, 2, 8, NB), bf16),
            pltpu.VMEM((2, chans + R, 2, 8, NB), bf16),
            pltpu.VMEM((4, tiles, 8, 256), f32),
            pltpu.VMEM((1, 2 * CB), jnp.int32),
            pltpu.VMEM((2, 2, 128, 128), f32),
            pltpu.VMEM((2, 16, 16, 128), f32),
            pltpu.VMEM((512, NLAG), bf16),
            pltpu.VMEM((512, NLAG), bf16),
            pltpu.VMEM((chans + 8, 1, 256), jnp.int32),
            pltpu.VMEM((256, tiles), bf16),
            pltpu.VMEM((tiles, 256), f32),
            pltpu.VMEM((4, tiles, 256), f32),
            pltpu.VMEM((2, tiles, 256), f32),
            pltpu.VMEM((2, chans, BIN_DEV, 256), bf16),
            pltpu.VMEM((2 * chans, BIN_DEV, 256), bf16),
            pltpu.VMEM((2, BIN_DEV, NLAG // 2), bf16),
            pltpu.VMEM((2, 4, BIN_DEV, NLAG // 2), bf16),
            dma((steps, 4)), dma((2,)), dma((steps,)), dma((steps,)), dma((steps,)),
            dma, dma, dma((2,)), dma((2,)), dma, dma, dma((2, 4)), dma((2, 4)),
            pltpu.SemaphoreType.REGULAR,
        ],
        compiler_params=pltpu.CompilerParams(
            collective_id=0, has_side_effects=True, vmem_limit_bytes=60 << 20
        ),
        name="stack",
    )(
        traces,
        *forward_factors(),
        *inverse_factors(),
        channel_mask.reshape(1, -1),
        owner_ids.reshape(1, -1),
        local_bins,
    )


def solution(mesh):
    in_specs = (P("seg", "chan", None), P("chan"), P("chan", None, None), P("chan", None))
    return jax.shard_map(
        per_device, mesh=mesh, in_specs=in_specs, out_specs=P("chan", None), check_vma=False
    )
```

```python
import functools
import math

import jax
import jax.numpy as jnp
import numpy as np
from jax import lax
from jax.experimental import pallas as pl
from jax.experimental.pallas import tpu as pltpu
from jax.sharding import PartitionSpec as P

CB = 128
NT = 4096
K0 = 8
HW = 64
R = 4
G = 16
BIN_DEV = 8
NB = 1024
NLAG = 2048
HALF = NB // 2
QUARTER = NT // 4
EPSILON = 1e-06
STEPS = ((0, 1), (1, 1), (2, 2), (4, 2), (6, 1), (7, 1))
MESH = pl.DeviceIdType.MESH


def forward_factors():
    freqs = K0 + np.arange(NB)
    unit = 2.0 * math.pi / NT
    coarse = (np.arange(16)[:, None, None] * 64 * freqs[None, None, :]) % NT * unit
    fine = (np.arange(64)[:, None] * freqs[None, :]) % NT * unit
    tables = (np.cos(coarse), -np.sin(coarse), np.cos(fine), -np.sin(fine))
    return [jnp.asarray(t, jnp.float32) for t in tables]


def inverse_factors():
    unit = 2.0 * math.pi / NT
    freqs = K0 + np.arange(NB)
    fine = (freqs[:, None] * np.arange(128)[None, :] * 2) % NT * unit
    coarse = (freqs[None, :16] * (np.arange(16)[:, None] * 128 - NLAG // 2) * 2) % NT * unit
    fine = np.stack([np.cos(fine), np.sin(fine)]).reshape(2, 2, 4, 128, 128)
    coarse = np.stack([np.cos(coarse), np.sin(coarse)]) / math.sqrt(NB)
    coarse = np.broadcast_to(coarse[..., None], (2, 16, 16, 128))
    return [jnp.asarray(fine, jnp.float32), jnp.asarray(coarse, jnp.float32)]


def peer(c, r):
    x, y, z = c % 2, (c // 2) % 4, c // 8
    return ((z + r % 4) % 4) * 8 + ((y + (r // 4) % 4) % 4) * 2 + (x + r // 16) % 2


def loop(first, last, body):
    def step(n, carry):
        body(n)
        return carry

    lax.fori_loop(first, last, step, 0)


def stack_kernel(
    total_segs,
    traces, coarse_re, coarse_im, fine_re, fine_im, inv_fine, inv_coarse_hbm, mask_row, owners, locals_,
    out_ref,
    x_ref, tab_0, tab_1, tab_2, tab_3, parts, spec, power, inv_level, valid_ref, send_one, recv_one, send_two, recv_two, acc,
    info_ref, fine_ref, inv_coarse, inv_hi, inv_lo, info, onehot, scale_ref, raw, raw_in, bins, bins_in, part, part_in,
    x_sem, fine_sem, own_sem, send_sem, recv_sem, info_send, info_recv, raw_send, raw_recv,
    bins_send, bins_recv, part_send, part_recv, entered,
):
    tab = (tab_0, tab_1, tab_2, tab_3)
    chans = lax.axis_size("chan")
    me = lax.axis_index("chan")
    seg = lax.axis_index("seg")
    other_core = seg + 1 - 2 * (seg % 2)
    other_chip = (seg + 2) % 4
    tiles = chans * R

    def load(i):
        at = pl.ds(*STEPS[i])
        return [
            pltpu.make_async_copy(
                traces.at[at, :, pl.ds(q * QUARTER, QUARTER)], x_ref.at[at, q], x_sem.at[i, q]
            )
            for q in range(4)
        ]

    def load_fine():
        return (
            pltpu.make_async_copy(inv_fine.at[:, :, seg], fine_ref, fine_sem.at[0]),
            pltpu.make_async_copy(inv_coarse_hbm, inv_coarse, fine_sem.at[1]),
        )

    for copy in load(0):
        copy.start()
    info_ref[:, pl.ds(0, CB)] = mask_row[...]
    info_ref[:, pl.ds(CB, CB)] = jnp.zeros((1, CB), jnp.int32)
    info_ref[:, pl.ds(CB, R * G)] = owners[...] * BIN_DEV + locals_[...]

    barrier = pltpu.get_barrier_semaphore()

    def greet(r):
        pl.semaphore_signal(barrier, inc=1, device_id={"chan": peer(me, r)}, device_id_type=MESH)

    for to in (other_core, other_chip):
        pl.semaphore_signal(barrier, inc=1, device_id={"seg": to}, device_id_type=MESH)

    def make_rows(a, half):
        at = pl.ds(a * 64 if isinstance(a, int) else pl.multiple_of(a * 64, 64), 64)
        for chunk in range(4 * half, 4 * half + 4):
            cols = pl.ds(chunk * 128, 128)
            ar, ai = coarse_re[a, :, cols], coarse_im[a, :, cols]
            br, bi = fine_re[:, cols], fine_im[:, cols]
            base = (chunk % 4) * 128
            tab[2 * half][at, pl.ds(base, 128)] = (ar * br - ai * bi).astype(jnp.bfloat16)
            tab[2 * half + 1][at, pl.ds(base, 128)] = (ar * bi + ai * br).astype(jnp.bfloat16)

    def first_half(a):
        greet(2 * a + 1)
        make_rows(a, 0)

    def first_half_and_greet(a):
        greet(2 * a + 2)
        first_half(a)

    loop(0, chans // 2 - 1, first_half_and_greet)
    first_half(chans // 2 - 1)

    turn = lax.broadcasted_iota(jnp.int32, (16, 256), 1) % 4
    c0 = jnp.where(turn == 0, 1.0, jnp.where(turn == 2, -1.0, 0.0))
    c1 = jnp.where(turn == 1, 1.0, jnp.where(turn == 3, -1.0, 0.0))
    flip = jnp.where(turn % 2 == 0, 1.0, -1.0)

    own = jnp.broadcast_to(info_ref[:, pl.ds(0, CB)].astype(jnp.float32), (CB, CB))
    diagonal = lax.broadcasted_iota(jnp.int32, (CB, CB), 0) == lax.broadcasted_iota(
        jnp.int32, (CB, CB), 1
    )
    column = jnp.sum(jnp.where(diagonal, own, 0.0), axis=1, keepdims=True)
    valid_ref[...] = jnp.broadcast_to(column, (CB, CB))

    power[:, pl.ds(0, 128)] = jnp.zeros((2 * CB, 128), jnp.bfloat16)
    power[:, pl.ds(128 + NB, 128)] = jnp.zeros((2 * CB, 128), jnp.bfloat16)
    near = (
        lax.broadcasted_iota(jnp.int32, (512, 256), 0)
        - lax.broadcasted_iota(jnp.int32, (512, 256), 1)
        - 128
    )
    band = jnp.where(jnp.abs(near) <= HW, 1.0, 0.0).astype(jnp.bfloat16)

    send = [send_one.at[0], send_one.at[1], send_two.at[0], send_two.at[1], send_one.at[2], send_one.at[3]]
    recv = [recv_one.at[0], recv_one.at[1], recv_two.at[0], recv_two.at[1], recv_one.at[2], recv_one.at[3]]

    def exchange(i, r):
        to = peer(me, r)
        return pltpu.make_async_remote_copy(
            send[i].at[to],
            recv[i].at[me],
            send_sem.at[i],
            recv_sem.at[i],
            device_id={"chan": to},
            device_id_type=MESH,
        )

    def keep(i):
        return pltpu.make_async_copy(send[i].at[me], recv[i].at[me], own_sem.at[i])

    def await_all(ref, sem):
        pieces = ref.at[pl.ds(0, chans - 1)]
        pltpu.make_async_copy(pieces, pieces, sem).wait()

    def tell(r):
        to = peer(me, r)
        return pltpu.make_async_remote_copy(
            info_ref,
            info.at[me],
            info_send,
            info_recv,
            device_id={"chan": to},
            device_id_type=MESH,
        )

    def await_step(ref, i, sem):
        pieces = ref[i].at[pl.ds(0, chans - 1)]
        pltpu.make_async_copy(pieces, pieces, sem.at[i]).wait()

    def whiten_step(i):
        first, segs = STEPS[i]
        rows = segs * CB
        every = pl.ds(0, rows)
        for copy in load(i):
            copy.wait()
        if i == 0:
            for copy in [copy for j in range(1, len(STEPS)) for copy in load(j)]:
                copy.start()
            for copy in load_fine():
                copy.start()

        def transform(n):
            block = x_ref[pl.ds(first, segs)].reshape(4 * rows, QUARTER)
            parts[pl.ds(0, 4 * rows), pl.ds(n * 512, 512)] = jnp.dot(
                block, tab[n][...], preferred_element_type=jnp.float32
            )

        for n in range(4):
            transform(n)
            if i == 0 and n < 2:
                for a in range(8 * n, 8 * n + 8):
                    make_rows(a, 1)

        def add_power(n):
            at = pl.ds(pl.multiple_of(n * 16, 16), 16)
            s, row = n // (CB // 16), n % (CB // 16)
            for chunk in range(NB // 256):
                base = (chunk // 2) * NB + (chunk % 2) * 256
                res, ims = [], []
                for q in range(4):
                    rows_of = pl.ds(pl.multiple_of((s * 4 + q) * CB + row * 16, 16), 16)
                    res.append(parts[rows_of, pl.ds(base, 256)])
                    ims.append(parts[rows_of, pl.ds(base + HALF, 256)])
                b_re, b_im = res[1] + flip * res[3], ims[1] + flip * ims[3]
                re = res[0] + flip * res[2] + (c0 * b_re + c1 * b_im)
                im = ims[0] + flip * ims[2] + (c0 * b_im - c1 * b_re)
                spec[at, pl.ds(base, 256)] = re
                spec[at, pl.ds(base + HALF, 256)] = im
                power[at, pl.ds(128 + chunk * 256, 256)] = (re * re + im * im).astype(jnp.bfloat16)

        loop(0, rows // 16, add_power)

        for chunk in range(NB // 256):
            total = jnp.dot(
                power[every, pl.ds(chunk * 256, 512)], band, preferred_element_type=jnp.float32
            )
            k = chunk * 256 + lax.broadcasted_iota(jnp.int32, (1, 256), 1)
            count = jnp.minimum(k + HW, NB - 1) - jnp.maximum(k - HW, 0) + 1
            inv_level[every, pl.ds(chunk * 256, 256)] = lax.rsqrt(
                total * (1.0 / count.astype(jnp.float32)) + EPSILON
            )

        def scale(g):
            valid = valid_ref[pl.ds(pl.multiple_of(g * 8, 8), 8), :]
            for s in range(segs):
                row = pl.ds(pl.multiple_of(s * CB + g * 8, 8), 8)
                for chunk in range(NB // 128):
                    h, at = chunk // 4, (chunk % 4) * 128
                    weight = inv_level[row, pl.ds(chunk * 128, 128)] * valid
                    re = spec[row, pl.ds(h * NB + at, 128)] * weight
                    im = spec[row, pl.ds(h * NB + HALF + at, 128)] * weight
                    to = 2 * g + h
                    block = send[i].at[to, s] if segs == 2 else send[i].at[to]
                    block[:, pl.ds(at, 128)] = re.astype(jnp.bfloat16)
                    block[:, pl.ds(HALF + at, 128)] = im.astype(jnp.bfloat16)

        loop(0, G, scale)
        keep(i).start()

    def send_step(i):
        loop(1, chans, lambda r: exchange(i, chans - r).start())

    whiten_step(0)
    pl.semaphore_wait(barrier, chans + 1)
    pl.semaphore_signal(entered, inc=1, device_id={"seg": other_chip}, device_id_type=MESH)
    send_step(0)
    for i in range(1, len(STEPS)):
        whiten_step(i)
        send_step(i)
        if i == 2:
            loop(1, chans, lambda r: tell(r).start())

    for block in recv:
        block[pl.ds(chans, R)] = jnp.zeros((R,) + block.shape[1:], jnp.bfloat16)
    for copy in load_fine():
        copy.wait()

    def make_inverse(n):
        h, at = n // 8, pl.multiple_of((n % 8) * 16, 16)
        br, bi = fine_ref[0, h, pl.ds(at, 16)], fine_ref[1, h, pl.ds(at, 16)]
        for a in range(16):
            ar, ai = inv_coarse[0, a], inv_coarse[1, a]
            re, im = ar * br - ai * bi, -(ar * bi + ai * br)
            for which, value in enumerate((re, im)):
                at_row = pl.ds(pl.multiple_of(h * 256 + which * 128 + at, 16), 16)
                high = value.astype(jnp.bfloat16)
                inv_hi[at_row, pl.ds(a * 128, 128)] = high
                low = value - high.astype(jnp.float32)
                inv_lo[at_row, pl.ds(a * 128, 128)] = low.astype(jnp.bfloat16)

    loop(0, 16, make_inverse)

    def products(steps, chunk, first, add=True):
        re_at = pl.ds(pl.multiple_of(chunk * 128, 128), 128)
        im_at = pl.ds(pl.multiple_of(HALF + chunk * 128, 128), 128)
        blocks = []
        for i in steps:
            two = STEPS[i][1] == 2
            for s in range(STEPS[i][1]):
                blocks.append(
                    [recv[i].at[first + j, s] if two else recv[i].at[first + j] for j in range(4 + R)]
                )
        re = [[ref[:, re_at].astype(jnp.float32) for ref in refs] for refs in blocks]
        im = [[ref[:, im_at].astype(jnp.float32) for ref in refs] for refs in blocks]
        for j in range(4):
            for d in range(1, R + 1):
                t = (d - 1) * chans + first + j
                p, q = (0.0, 0.0) if not add else (
                    acc[chunk, t, :, pl.ds(0, 128)], acc[chunk, t, :, pl.ds(128, 128)]
                )
                for s in range(len(blocks)):
                    p = p + (re[s][j] * re[s][j + d] + im[s][j] * im[s][j + d])
                    q = q + (im[s][j] * re[s][j + d] - re[s][j] * im[s][j + d])
                acc[chunk, t, :, pl.ds(0, 128)] = p
                acc[chunk, t, :, pl.ds(128, 128)] = q

    def here(i):
        await_step(recv, i, recv_sem)
        keep(i).wait()

    here(0)
    here(1)
    loop(0, chans, lambda n: products((0, 1), n % 4, (n // 4) * 4, add=False))
    for i in (2, 3, 4):
        here(i)
        loop(0, chans, lambda n: products((i,), n % 4, (n // 4) * 4))

    info[pl.ds(me, 1)] = info_ref[...].reshape(1, 1, 256)
    info[pl.ds(chans, 8)] = jnp.zeros((8, 1, 256), jnp.int32)
    await_all(info, info_recv)
    group = me // 2
    lanes = lax.broadcasted_iota(jnp.int32, (chans, CB), 1)
    everyone = info[...].reshape(chans + 8, 256).astype(jnp.float32)
    masks, names = everyone[:, :CB], everyone[:chans, CB:]
    picked = []
    for d in range(1, R + 1):
        both = masks[:chans] * masks[d : d + chans]
        count = jnp.sum(jnp.where(lanes // 8 == group, both, 0.0), axis=1, keepdims=True)
        factor = 1.0 / (total_segs * jnp.maximum(count, 1.0))
        scale_ref[pl.ds((d - 1) * chans, chans), :] = jnp.broadcast_to(factor, (chans, 256))
        mine = lanes == (d - 1) * G + group
        name = jnp.sum(jnp.where(mine, names, 0.0), axis=1, keepdims=True)
        bin_of = lax.broadcasted_iota(jnp.int32, (chans, 256), 1).astype(jnp.float32)
        picked.append(jnp.where(jnp.broadcast_to(name, (chans, 256)) == bin_of, 1.0, 0.0))
    onehot[...] = jnp.concatenate(picked, 0).T.astype(jnp.bfloat16)

    here(len(STEPS) - 1)

    def hand_over(n, chunk):
        return pltpu.make_async_remote_copy(
            raw.at[chunk],
            raw_in.at[n],
            raw_send.at[n],
            raw_recv.at[n],
            device_id={"seg": other_core},
            device_id_type=MESH,
        )

    def finish_quarter(chunk):
        loop(0, chans // 4, lambda n: products((len(STEPS) - 1,), chunk, n * 4))

        def reduce_rows(n):
            at = pl.ds(pl.multiple_of(n * 8, 8), 8)
            raw[chunk, at, :] = acc[chunk, at].sum(1)

        loop(0, tiles // 8, reduce_rows)

    chip = seg - seg % 2
    far = 2 - chip

    def give(n, chunk):
        finish_quarter(chunk)
        hand_over(n, chunk).start()

    def stack(n, sums):
        sums = sums * scale_ref[...]
        high = sums.astype(jnp.bfloat16)
        low = (sums - high.astype(jnp.float32)).astype(jnp.bfloat16)
        stacked = jnp.dot(onehot[...], high, preferred_element_type=jnp.float32)
        stacked += jnp.dot(onehot[...], low, preferred_element_type=jnp.float32)
        bins[n] = stacked.reshape(chans, BIN_DEV, 256).astype(jnp.bfloat16)

    def deliver(n, r):
        to = peer(me, r)
        return pltpu.make_async_remote_copy(
            bins.at[n, to],
            bins_in.at[n * chans + me],
            bins_send,
            bins_recv,
            device_id={"seg": other_chip if n else seg, "chan": to},
            device_id_type=MESH,
        )

    give(0, far + other_core % 2)
    finish_quarter(other_chip)
    give(1, other_core)
    hand_over(0, far + other_core % 2).wait()
    stack(1, raw[other_chip] + raw_in[0])
    pl.semaphore_wait(entered, 1)
    loop(0, chans, lambda r: deliver(1, chans - 1 - r).start())
    finish_quarter(seg)
    hand_over(1, other_core).wait()
    stack(0, raw[seg] + raw_in[1])
    loop(1, chans, lambda r: deliver(0, chans - r).start())
    bins_in[me] = bins[0, me]
    pieces = bins_in.at[pl.ds(0, 2 * chans - 1)]
    pltpu.make_async_copy(pieces, pieces, bins_recv).wait()
    halves = []
    for h in range(2):
        total = bins_in[h].astype(jnp.float32)
        for g in range(1, 2 * G):
            total = total + bins_in[2 * g + h].astype(jnp.float32)
        halves.append(total)
    spectra = jnp.concatenate(halves, axis=1)
    high = spectra.astype(jnp.bfloat16)
    low = (spectra - high.astype(jnp.float32)).astype(jnp.bfloat16)
    both = jnp.concatenate([high, low], axis=0)

    def share(n, q):
        return pltpu.make_async_remote_copy(
            part.at[n],
            part_in.at[n, seg],
            part_send.at[n, q],
            part_recv.at[n, seg],
            device_id={"seg": (seg + q) % 4},
            device_id_type=MESH,
        )

    width = NLAG // 2
    for n in range(2):
        at = pl.ds(n * width, width)
        value = jnp.dot(both, inv_hi[:, at], preferred_element_type=jnp.float32)
        value = value[:BIN_DEV] + value[BIN_DEV:]
        value += jnp.dot(high, inv_lo[:, at], preferred_element_type=jnp.float32)
        part[n] = value.astype(jnp.bfloat16)
        for q in (2, 1, 3):
            share(n, q).start()
        part_in[n, seg] = value.astype(jnp.bfloat16)
    for n in range(2):
        for q in (1, 2, 3):
            source = part_in.at[n, (seg + q) % 4]
            pltpu.make_async_copy(source, source, part_recv.at[n, (seg + q) % 4]).wait()
        terms = [part_in[n, q].astype(jnp.float32) for q in range(4)]
        out_ref[:, pl.ds(n * width, width)] = (terms[0] + terms[1]) + (terms[2] + terms[3])

    for n in range(2):
        for q in (1, 2, 3):
            share(n, q).wait_send()
    for i in range(len(STEPS)):
        await_step(send, i, send_sem)
    await_all(info, info_send)
    pltpu.make_async_copy(pieces, pieces, bins_send).wait()


def per_device(traces, channel_mask, owner_ids, local_bins):
    chans, quarters = lax.axis_size("chan"), lax.axis_size("seg")
    tiles, steps = chans * R, len(STEPS)
    vmem = pl.BlockSpec(memory_space=pltpu.VMEM)
    anywhere = pl.BlockSpec(memory_space=pl.ANY)
    dma = pltpu.SemaphoreType.DMA
    bf16, f32 = jnp.bfloat16, jnp.float32
    return pl.pallas_call(
        functools.partial(stack_kernel, float(traces.shape[0] * quarters)),
        out_shape=jax.ShapeDtypeStruct((BIN_DEV, NLAG), f32),
        in_specs=[anywhere] + [vmem] * 4 + [anywhere] * 2 + [vmem] * 3,
        out_specs=vmem,
        scratch_shapes=[
            pltpu.VMEM((traces.shape[0], 4, CB, QUARTER), bf16),
            *[pltpu.VMEM((QUARTER, 512), bf16)] * 4,
            pltpu.VMEM((8 * CB, 2 * NB), f32),
            pltpu.VMEM((2 * CB, 2 * NB), f32),
            pltpu.VMEM((2 * CB, NB + 256), bf16),
            pltpu.VMEM((2 * CB, NB), f32),
            pltpu.VMEM((CB, CB), f32),
            pltpu.VMEM((4, chans, 8, NB), bf16),
            pltpu.VMEM((4, chans + R, 8, NB), bf16),
            pltpu.VMEM((2, chans, 2, 8, NB), bf16),
            pltpu.VMEM((2, chans + R, 2, 8, NB), bf16),
            pltpu.VMEM((4, tiles, 8, 256), f32),
            pltpu.VMEM((1, 2 * CB), jnp.int32),
            pltpu.VMEM((2, 2, 128, 128), f32),
            pltpu.VMEM((2, 16, 16, 128), f32),
            pltpu.VMEM((512, NLAG), bf16),
            pltpu.VMEM((512, NLAG), bf16),
            pltpu.VMEM((chans + 8, 1, 256), jnp.int32),
            pltpu.VMEM((256, tiles), bf16),
            pltpu.VMEM((tiles, 256), f32),
            pltpu.VMEM((4, tiles, 256), f32),
            pltpu.VMEM((2, tiles, 256), f32),
            pltpu.VMEM((2, chans, BIN_DEV, 256), bf16),
            pltpu.VMEM((2 * chans, BIN_DEV, 256), bf16),
            pltpu.VMEM((2, BIN_DEV, NLAG // 2), bf16),
            pltpu.VMEM((2, 4, BIN_DEV, NLAG // 2), bf16),
            dma((steps, 4)), dma((2,)), dma((steps,)), dma((steps,)), dma((steps,)),
            dma, dma, dma((2,)), dma((2,)), dma, dma, dma((2, 4)), dma((2, 4)),
            pltpu.SemaphoreType.REGULAR,
        ],
        compiler_params=pltpu.CompilerParams(
            collective_id=0, has_side_effects=True, vmem_limit_bytes=60 << 20
        ),
        name="stack",
    )(
        traces,
        *forward_factors(),
        *inverse_factors(),
        channel_mask.reshape(1, -1),
        owner_ids.reshape(1, -1),
        local_bins,
    )


def solution(mesh):
    in_specs = (P("seg", "chan", None), P("chan"), P("chan", None, None), P("chan", None))
    return jax.shard_map(
        per_device, mesh=mesh, in_specs=in_specs, out_specs=P("chan", None), check_vma=False
    )
```

```python
import functools
import math

import jax
import jax.numpy as jnp
import numpy as np
from jax import lax
from jax.experimental import pallas as pl
from jax.experimental.pallas import tpu as pltpu
from jax.sharding import PartitionSpec as P

CB = 128
NT = 4096
K0 = 8
HW = 64
R = 4
G = 16
BIN_DEV = 8
NB = 1024
NLAG = 2048
HALF = NB // 2
QUARTER = NT // 4
EPSILON = 1e-06
STEPS = ((0, 1), (1, 1), (2, 2), (4, 2), (6, 1), (7, 1))
MESH = pl.DeviceIdType.MESH


def forward_factors():
    freqs = K0 + np.arange(NB)
    unit = 2.0 * math.pi / NT
    coarse = (np.arange(16)[:, None, None] * 64 * freqs[None, None, :]) % NT * unit
    fine = (np.arange(64)[:, None] * freqs[None, :]) % NT * unit
    tables = (np.cos(coarse), -np.sin(coarse), np.cos(fine), -np.sin(fine))
    return [jnp.asarray(t, jnp.float32) for t in tables]


def inverse_factors():
    unit = 2.0 * math.pi / NT
    freqs = K0 + np.arange(NB)
    fine = (freqs[:, None] * np.arange(128)[None, :] * 2) % NT * unit
    coarse = (freqs[None, :16] * (np.arange(16)[:, None] * 128 - NLAG // 2) * 2) % NT * unit
    fine = np.stack([np.cos(fine), np.sin(fine)]).reshape(2, 2, 4, 128, 128)
    coarse = np.stack([np.cos(coarse), np.sin(coarse)]) / math.sqrt(NB)
    coarse = np.broadcast_to(coarse[..., None], (2, 16, 16, 128))
    return [jnp.asarray(fine, jnp.float32), jnp.asarray(coarse, jnp.float32)]


def peer(c, r):
    x, y, z = c % 2, (c // 2) % 4, c // 8
    return ((z + r % 4) % 4) * 8 + ((y + (r // 4) % 4) % 4) * 2 + (x + r // 16) % 2


def loop(first, last, body):
    def step(n, carry):
        body(n)
        return carry

    lax.fori_loop(first, last, step, 0)


def stack_kernel(
    total_segs,
    traces, coarse_re, coarse_im, fine_re, fine_im, inv_fine, inv_coarse_hbm, mask_row, owners, locals_,
    out_ref,
    x_ref, tab_0, tab_1, tab_2, tab_3, parts, spec, power, inv_level, valid_ref, send_one, recv_one, send_two, recv_two, acc,
    info_ref, fine_ref, inv_coarse, inv_hi, inv_lo, info, onehot, scale_ref, raw, raw_in, bins, bins_in, part, part_in,
    x_sem, fine_sem, own_sem, send_sem, recv_sem, info_send, info_recv, raw_send, raw_recv,
    bins_send, bins_recv, part_send, part_recv, entered,
):
    tab = (tab_0, tab_1, tab_2, tab_3)
    chans = lax.axis_size("chan")
    me = lax.axis_index("chan")
    seg = lax.axis_index("seg")
    other_core = seg + 1 - 2 * (seg % 2)
    other_chip = (seg + 2) % 4
    tiles = chans * R

    def load(i):
        at = pl.ds(*STEPS[i])
        return [
            pltpu.make_async_copy(
                traces.at[at, :, pl.ds(q * QUARTER, QUARTER)], x_ref.at[at, q], x_sem.at[i, q]
            )
            for q in range(4)
        ]

    def load_fine():
        return (
            pltpu.make_async_copy(inv_fine.at[:, :, seg], fine_ref, fine_sem.at[0]),
            pltpu.make_async_copy(inv_coarse_hbm, inv_coarse, fine_sem.at[1]),
        )

    for copy in load(0):
        copy.start()
    info_ref[:, pl.ds(0, CB)] = mask_row[...]
    info_ref[:, pl.ds(CB, CB)] = jnp.zeros((1, CB), jnp.int32)
    info_ref[:, pl.ds(CB, R * G)] = owners[...] * BIN_DEV + locals_[...]

    barrier = pltpu.get_barrier_semaphore()

    def greet(r):
        pl.semaphore_signal(barrier, inc=1, device_id={"chan": peer(me, r)}, device_id_type=MESH)

    for to in (other_core, other_chip):
        pl.semaphore_signal(barrier, inc=1, device_id={"seg": to}, device_id_type=MESH)

    for distance in range(1, chans):
        greet(distance)

    def make_rows(a, half):
        at = pl.ds(a * 64 if isinstance(a, int) else pl.multiple_of(a * 64, 64), 64)
        for chunk in range(4 * half, 4 * half + 4):
            cols = pl.ds(chunk * 128, 128)
            ar, ai = coarse_re[a, :, cols], coarse_im[a, :, cols]
            br, bi = fine_re[:, cols], fine_im[:, cols]
            base = (chunk % 4) * 128
            tab[2 * half][at, pl.ds(base, 128)] = (ar * br - ai * bi).astype(jnp.bfloat16)
            tab[2 * half + 1][at, pl.ds(base, 128)] = (ar * bi + ai * br).astype(jnp.bfloat16)

    loop(0, QUARTER // 64, lambda a: make_rows(a, 0))

    turn = lax.broadcasted_iota(jnp.int32, (16, 256), 1) % 4
    c0 = jnp.where(turn == 0, 1.0, jnp.where(turn == 2, -1.0, 0.0))
    c1 = jnp.where(turn == 1, 1.0, jnp.where(turn == 3, -1.0, 0.0))
    flip = jnp.where(turn % 2 == 0, 1.0, -1.0)

    own = jnp.broadcast_to(info_ref[:, pl.ds(0, CB)].astype(jnp.float32), (CB, CB))
    diagonal = lax.broadcasted_iota(jnp.int32, (CB, CB), 0) == lax.broadcasted_iota(
        jnp.int32, (CB, CB), 1
    )
    column = jnp.sum(jnp.where(diagonal, own, 0.0), axis=1, keepdims=True)
    valid_ref[...] = jnp.broadcast_to(column, (CB, CB))

    power[:, pl.ds(0, 128)] = jnp.zeros((2 * CB, 128), jnp.bfloat16)
    power[:, pl.ds(128 + NB, 128)] = jnp.zeros((2 * CB, 128), jnp.bfloat16)
    near = (
        lax.broadcasted_iota(jnp.int32, (512, 256), 0)
        - lax.broadcasted_iota(jnp.int32, (512, 256), 1)
        - 128
    )
    band = jnp.where(jnp.abs(near) <= HW, 1.0, 0.0).astype(jnp.bfloat16)

    send = [send_one.at[0], send_one.at[1], send_two.at[0], send_two.at[1], send_one.at[2], send_one.at[3]]
    recv = [recv_one.at[0], recv_one.at[1], recv_two.at[0], recv_two.at[1], recv_one.at[2], recv_one.at[3]]

    def exchange(i, r):
        to = peer(me, r)
        return pltpu.make_async_remote_copy(
            send[i].at[to],
            recv[i].at[me],
            send_sem.at[i],
            recv_sem.at[i],
            device_id={"chan": to},
            device_id_type=MESH,
        )

    def keep(i):
        return pltpu.make_async_copy(send[i].at[me], recv[i].at[me], own_sem.at[i])

    def await_all(ref, sem):
        pieces = ref.at[pl.ds(0, chans - 1)]
        pltpu.make_async_copy(pieces, pieces, sem).wait()

    def tell(r):
        to = peer(me, r)
        return pltpu.make_async_remote_copy(
            info_ref,
            info.at[me],
            info_send,
            info_recv,
            device_id={"chan": to},
            device_id_type=MESH,
        )

    def await_step(ref, i, sem):
        pieces = ref[i].at[pl.ds(0, chans - 1)]
        pltpu.make_async_copy(pieces, pieces, sem.at[i]).wait()

    def whiten_step(i):
        first, segs = STEPS[i]
        rows = segs * CB
        every = pl.ds(0, rows)
        for copy in load(i):
            copy.wait()
        if i == 0:
            for copy in [copy for j in range(1, len(STEPS)) for copy in load(j)]:
                copy.start()
            for copy in load_fine():
                copy.start()

        def transform(n):
            block = x_ref[pl.ds(first, segs)].reshape(4 * rows, QUARTER)
            parts[pl.ds(0, 4 * rows), pl.ds(n * 512, 512)] = jnp.dot(
                block, tab[n][...], preferred_element_type=jnp.float32
            )

        for n in range(4):
            transform(n)
            if i == 0 and n < 2:
                for a in range(8 * n, 8 * n + 8):
                    make_rows(a, 1)

        def add_power(n):
            at = pl.ds(pl.multiple_of(n * 16, 16), 16)
            s, row = n // (CB // 16), n % (CB // 16)
            for chunk in range(NB // 256):
                base = (chunk // 2) * NB + (chunk % 2) * 256
                res, ims = [], []
                for q in range(4):
                    rows_of = pl.ds(pl.multiple_of((s * 4 + q) * CB + row * 16, 16), 16)
                    res.append(parts[rows_of, pl.ds(base, 256)])
                    ims.append(parts[rows_of, pl.ds(base + HALF, 256)])
                b_re, b_im = res[1] + flip * res[3], ims[1] + flip * ims[3]
                re = res[0] + flip * res[2] + (c0 * b_re + c1 * b_im)
                im = ims[0] + flip * ims[2] + (c0 * b_im - c1 * b_re)
                spec[at, pl.ds(base, 256)] = re
                spec[at, pl.ds(base + HALF, 256)] = im
                power[at, pl.ds(128 + chunk * 256, 256)] = (re * re + im * im).astype(jnp.bfloat16)

        loop(0, rows // 16, add_power)

        for chunk in range(NB // 256):
            total = jnp.dot(
                power[every, pl.ds(chunk * 256, 512)], band, preferred_element_type=jnp.float32
            )
            k = chunk * 256 + lax.broadcasted_iota(jnp.int32, (1, 256), 1)
            count = jnp.minimum(k + HW, NB - 1) - jnp.maximum(k - HW, 0) + 1
            inv_level[every, pl.ds(chunk * 256, 256)] = lax.rsqrt(
                total * (1.0 / count.astype(jnp.float32)) + EPSILON
            )

        def scale(g):
            valid = valid_ref[pl.ds(pl.multiple_of(g * 8, 8), 8), :]
            for s in range(segs):
                row = pl.ds(pl.multiple_of(s * CB + g * 8, 8), 8)
                for chunk in range(NB // 128):
                    h, at = chunk // 4, (chunk % 4) * 128
                    weight = inv_level[row, pl.ds(chunk * 128, 128)] * valid
                    re = spec[row, pl.ds(h * NB + at, 128)] * weight
                    im = spec[row, pl.ds(h * NB + HALF + at, 128)] * weight
                    to = 2 * g + h
                    block = send[i].at[to, s] if segs == 2 else send[i].at[to]
                    block[:, pl.ds(at, 128)] = re.astype(jnp.bfloat16)
                    block[:, pl.ds(HALF + at, 128)] = im.astype(jnp.bfloat16)

        loop(0, G, scale)
        keep(i).start()

    def send_step(i):
        loop(1, chans, lambda r: exchange(i, chans - r).start())

    whiten_step(0)
    pl.semaphore_wait(barrier, chans + 1)
    pl.semaphore_signal(entered, inc=1, device_id={"seg": other_chip}, device_id_type=MESH)
    send_step(0)
    for i in range(1, len(STEPS)):
        whiten_step(i)
        send_step(i)
        if i == 2:
            loop(1, chans, lambda r: tell(r).start())

    for block in recv:
        block[pl.ds(chans, R)] = jnp.zeros((R,) + block.shape[1:], jnp.bfloat16)
    for copy in load_fine():
        copy.wait()

    def make_inverse(n):
        h, at = n // 8, pl.multiple_of((n % 8) * 16, 16)
        br, bi = fine_ref[0, h, pl.ds(at, 16)], fine_ref[1, h, pl.ds(at, 16)]
        for a in range(16):
            ar, ai = inv_coarse[0, a], inv_coarse[1, a]
            re, im = ar * br - ai * bi, -(ar * bi + ai * br)
            for which, value in enumerate((re, im)):
                at_row = pl.ds(pl.multiple_of(h * 256 + which * 128 + at, 16), 16)
                high = value.astype(jnp.bfloat16)
                inv_hi[at_row, pl.ds(a * 128, 128)] = high
                low = value - high.astype(jnp.float32)
                inv_lo[at_row, pl.ds(a * 128, 128)] = low.astype(jnp.bfloat16)

    loop(0, 16, make_inverse)

    def products(steps, chunk, first, add=True):
        re_at = pl.ds(pl.multiple_of(chunk * 128, 128), 128)
        im_at = pl.ds(pl.multiple_of(HALF + chunk * 128, 128), 128)
        blocks = []
        for i in steps:
            two = STEPS[i][1] == 2
            for s in range(STEPS[i][1]):
                blocks.append(
                    [recv[i].at[first + j, s] if two else recv[i].at[first + j] for j in range(4 + R)]
                )
        re = [[ref[:, re_at].astype(jnp.float32) for ref in refs] for refs in blocks]
        im = [[ref[:, im_at].astype(jnp.float32) for ref in refs] for refs in blocks]
        for j in range(4):
            for d in range(1, R + 1):
                t = (d - 1) * chans + first + j
                p, q = (0.0, 0.0) if not add else (
                    acc[chunk, t, :, pl.ds(0, 128)], acc[chunk, t, :, pl.ds(128, 128)]
                )
                for s in range(len(blocks)):
                    p = p + (re[s][j] * re[s][j + d] + im[s][j] * im[s][j + d])
                    q = q + (im[s][j] * re[s][j + d] - re[s][j] * im[s][j + d])
                acc[chunk, t, :, pl.ds(0, 128)] = p
                acc[chunk, t, :, pl.ds(128, 128)] = q

    def here(i):
        await_step(recv, i, recv_sem)
        keep(i).wait()

    here(0)
    here(1)
    loop(0, chans, lambda n: products((0, 1), n % 4, (n // 4) * 4, add=False))
    for i in (2, 3, 4):
        here(i)
        loop(0, chans, lambda n: products((i,), n % 4, (n // 4) * 4))

    info[pl.ds(me, 1)] = info_ref[...].reshape(1, 1, 256)
    info[pl.ds(chans, 8)] = jnp.zeros((8, 1, 256), jnp.int32)
    await_all(info, info_recv)
    group = me // 2
    lanes = lax.broadcasted_iota(jnp.int32, (chans, CB), 1)
    everyone = info[...].reshape(chans + 8, 256).astype(jnp.float32)
    masks, names = everyone[:, :CB], everyone[:chans, CB:]
    picked = []
    for d in range(1, R + 1):
        both = masks[:chans] * masks[d : d + chans]
        count = jnp.sum(jnp.where(lanes // 8 == group, both, 0.0), axis=1, keepdims=True)
        factor = 1.0 / (total_segs * jnp.maximum(count, 1.0))
        scale_ref[pl.ds((d - 1) * chans, chans), :] = jnp.broadcast_to(factor, (chans, 256))
        mine = lanes == (d - 1) * G + group
        name = jnp.sum(jnp.where(mine, names, 0.0), axis=1, keepdims=True)
        bin_of = lax.broadcasted_iota(jnp.int32, (chans, 256), 1).astype(jnp.float32)
        picked.append(jnp.where(jnp.broadcast_to(name, (chans, 256)) == bin_of, 1.0, 0.0))
    onehot[...] = jnp.concatenate(picked, 0).T.astype(jnp.bfloat16)

    here(len(STEPS) - 1)

    def hand_over(n, chunk):
        return pltpu.make_async_remote_copy(
            raw.at[chunk],
            raw_in.at[n],
            raw_send.at[n],
            raw_recv.at[n],
            device_id={"seg": other_core},
            device_id_type=MESH,
        )

    def finish_quarter(chunk):
        loop(0, chans // 4, lambda n: products((len(STEPS) - 1,), chunk, n * 4))

        def reduce_rows(n):
            at = pl.ds(pl.multiple_of(n * 8, 8), 8)
            raw[chunk, at, :] = acc[chunk, at].sum(1)

        loop(0, tiles // 8, reduce_rows)

    chip = seg - seg % 2
    far = 2 - chip

    def give(n, chunk):
        finish_quarter(chunk)
        hand_over(n, chunk).start()

    def stack(n, sums):
        sums = sums * scale_ref[...]
        high = sums.astype(jnp.bfloat16)
        low = (sums - high.astype(jnp.float32)).astype(jnp.bfloat16)
        stacked = jnp.dot(onehot[...], high, preferred_element_type=jnp.float32)
        stacked += jnp.dot(onehot[...], low, preferred_element_type=jnp.float32)
        bins[n] = stacked.reshape(chans, BIN_DEV, 256).astype(jnp.bfloat16)

    def deliver(n, r):
        to = peer(me, r)
        return pltpu.make_async_remote_copy(
            bins.at[n, to],
            bins_in.at[n * chans + me],
            bins_send,
            bins_recv,
            device_id={"seg": other_chip if n else seg, "chan": to},
            device_id_type=MESH,
        )

    give(0, far + other_core % 2)
    finish_quarter(other_chip)
    give(1, other_core)
    hand_over(0, far + other_core % 2).wait()
    stack(1, raw[other_chip] + raw_in[0])
    pl.semaphore_wait(entered, 1)
    loop(0, chans, lambda r: deliver(1, chans - 1 - r).start())
    finish_quarter(seg)
    hand_over(1, other_core).wait()
    stack(0, raw[seg] + raw_in[1])
    loop(1, chans, lambda r: deliver(0, chans - r).start())
    bins_in[me] = bins[0, me]
    pieces = bins_in.at[pl.ds(0, 2 * chans - 1)]
    pltpu.make_async_copy(pieces, pieces, bins_recv).wait()
    halves = []
    for h in range(2):
        total = bins_in[h].astype(jnp.float32)
        for g in range(1, 2 * G):
            total = total + bins_in[2 * g + h].astype(jnp.float32)
        halves.append(total)
    spectra = jnp.concatenate(halves, axis=1)
    high = spectra.astype(jnp.bfloat16)
    low = (spectra - high.astype(jnp.float32)).astype(jnp.bfloat16)
    both = jnp.concatenate([high, low], axis=0)

    def share(n, q):
        return pltpu.make_async_remote_copy(
            part.at[n],
            part_in.at[n, seg],
            part_send.at[n, q],
            part_recv.at[n, seg],
            device_id={"seg": (seg + q) % 4},
            device_id_type=MESH,
        )

    width = NLAG // 2
    for n in range(2):
        at = pl.ds(n * width, width)
        value = jnp.dot(both, inv_hi[:, at], preferred_element_type=jnp.float32)
        value = value[:BIN_DEV] + value[BIN_DEV:]
        value += jnp.dot(high, inv_lo[:, at], preferred_element_type=jnp.float32)
        part[n] = value.astype(jnp.bfloat16)
        for q in (2, 1, 3):
            share(n, q).start()
        part_in[n, seg] = value.astype(jnp.bfloat16)
    for n in range(2):
        for q in (1, 2, 3):
            source = part_in.at[n, (seg + q) % 4]
            pltpu.make_async_copy(source, source, part_recv.at[n, (seg + q) % 4]).wait()
        terms = [part_in[n, q].astype(jnp.float32) for q in range(4)]
        out_ref[:, pl.ds(n * width, width)] = (terms[0] + terms[1]) + (terms[2] + terms[3])

    for n in range(2):
        for q in (1, 2, 3):
            share(n, q).wait_send()
    for i in range(len(STEPS)):
        await_step(send, i, send_sem)
    await_all(info, info_send)
    pltpu.make_async_copy(pieces, pieces, bins_send).wait()


def per_device(traces, channel_mask, owner_ids, local_bins):
    chans, quarters = lax.axis_size("chan"), lax.axis_size("seg")
    tiles, steps = chans * R, len(STEPS)
    vmem = pl.BlockSpec(memory_space=pltpu.VMEM)
    anywhere = pl.BlockSpec(memory_space=pl.ANY)
    dma = pltpu.SemaphoreType.DMA
    bf16, f32 = jnp.bfloat16, jnp.float32
    return pl.pallas_call(
        functools.partial(stack_kernel, float(traces.shape[0] * quarters)),
        out_shape=jax.ShapeDtypeStruct((BIN_DEV, NLAG), f32),
        in_specs=[anywhere] + [vmem] * 4 + [anywhere] * 2 + [vmem] * 3,
        out_specs=vmem,
        scratch_shapes=[
            pltpu.VMEM((traces.shape[0], 4, CB, QUARTER), bf16),
            *[pltpu.VMEM((QUARTER, 512), bf16)] * 4,
            pltpu.VMEM((8 * CB, 2 * NB), f32),
            pltpu.VMEM((2 * CB, 2 * NB), f32),
            pltpu.VMEM((2 * CB, NB + 256), bf16),
            pltpu.VMEM((2 * CB, NB), f32),
            pltpu.VMEM((CB, CB), f32),
            pltpu.VMEM((4, chans, 8, NB), bf16),
            pltpu.VMEM((4, chans + R, 8, NB), bf16),
            pltpu.VMEM((2, chans, 2, 8, NB), bf16),
            pltpu.VMEM((2, chans + R, 2, 8, NB), bf16),
            pltpu.VMEM((4, tiles, 8, 256), f32),
            pltpu.VMEM((1, 2 * CB), jnp.int32),
            pltpu.VMEM((2, 2, 128, 128), f32),
            pltpu.VMEM((2, 16, 16, 128), f32),
            pltpu.VMEM((512, NLAG), bf16),
            pltpu.VMEM((512, NLAG), bf16),
            pltpu.VMEM((chans + 8, 1, 256), jnp.int32),
            pltpu.VMEM((256, tiles), bf16),
            pltpu.VMEM((tiles, 256), f32),
            pltpu.VMEM((4, tiles, 256), f32),
            pltpu.VMEM((2, tiles, 256), f32),
            pltpu.VMEM((2, chans, BIN_DEV, 256), bf16),
            pltpu.VMEM((2 * chans, BIN_DEV, 256), bf16),
            pltpu.VMEM((2, BIN_DEV, NLAG // 2), bf16),
            pltpu.VMEM((2, 4, BIN_DEV, NLAG // 2), bf16),
            dma((steps, 4)), dma((2,)), dma((steps,)), dma((steps,)), dma((steps,)),
            dma, dma, dma((2,)), dma((2,)), dma, dma, dma((2, 4)), dma((2, 4)),
            pltpu.SemaphoreType.REGULAR,
        ],
        compiler_params=pltpu.CompilerParams(
            collective_id=0, has_side_effects=True, vmem_limit_bytes=60 << 20
        ),
        name="stack",
    )(
        traces,
        *forward_factors(),
        *inverse_factors(),
        channel_mask.reshape(1, -1),
        owner_ids.reshape(1, -1),
        local_bins,
    )


def solution(mesh):
    in_specs = (P("seg", "chan", None), P("chan"), P("chan", None, None), P("chan", None))
    return jax.shard_map(
        per_device, mesh=mesh, in_specs=in_specs, out_specs=P("chan", None), check_vma=False
    )
```

```python
import functools
import math

import jax
import jax.numpy as jnp
import numpy as np
from jax import lax
from jax.experimental import pallas as pl
from jax.experimental.pallas import tpu as pltpu
from jax.sharding import PartitionSpec as P

CB = 128
NT = 4096
K0 = 8
HW = 64
R = 4
G = 16
BIN_DEV = 8
NB = 1024
NLAG = 2048
HALF = NB // 2
QUARTER = NT // 4
EPSILON = 1e-06
STEPS = ((0, 1), (1, 1), (2, 2), (4, 2), (6, 1), (7, 1))
MESH = pl.DeviceIdType.MESH


def forward_factors():
    freqs = K0 + np.arange(NB)
    unit = 2.0 * math.pi / NT
    coarse = (np.arange(16)[:, None, None] * 64 * freqs[None, None, :]) % NT * unit
    fine = (np.arange(64)[:, None] * freqs[None, :]) % NT * unit
    tables = (np.cos(coarse), -np.sin(coarse), np.cos(fine), -np.sin(fine))
    return [jnp.asarray(t, jnp.float32) for t in tables]


def inverse_factors():
    unit = 2.0 * math.pi / NT
    freqs = K0 + np.arange(NB)
    fine = (freqs[:, None] * np.arange(128)[None, :] * 2) % NT * unit
    coarse = (freqs[None, :16] * (np.arange(16)[:, None] * 128 - NLAG // 2) * 2) % NT * unit
    fine = np.stack([np.cos(fine), np.sin(fine)]).reshape(2, 2, 4, 128, 128)
    coarse = np.stack([np.cos(coarse), np.sin(coarse)]) / math.sqrt(NB)
    coarse = np.broadcast_to(coarse[..., None], (2, 16, 16, 128))
    return [jnp.asarray(fine, jnp.float32), jnp.asarray(coarse, jnp.float32)]


def peer(c, r):
    x, y, z = c % 2, (c // 2) % 4, c // 8
    return ((z + r % 4) % 4) * 8 + ((y + (r // 4) % 4) % 4) * 2 + (x + r // 16) % 2


def loop(first, last, body):
    def step(n, carry):
        body(n)
        return carry

    lax.fori_loop(first, last, step, 0)


def stack_kernel(
    total_segs,
    traces, coarse_re, coarse_im, fine_re, fine_im, inv_fine, inv_coarse_hbm, mask_row, owners, locals_,
    out_ref,
    x_ref, tab_0, tab_1, tab_2, tab_3, parts, spec, power, inv_level, valid_ref, send_one, recv_one, send_two, recv_two, acc,
    info_ref, fine_ref, inv_coarse, inv_hi, inv_lo, info, onehot, scale_ref, raw, raw_in, bins, bins_in, part, part_in,
    x_sem, fine_sem, own_sem, send_sem, recv_sem, info_send, info_recv, raw_send, raw_recv,
    bins_send, bins_recv, part_send, part_recv, entered,
):
    tab = (tab_0, tab_1, tab_2, tab_3)
    chans = lax.axis_size("chan")
    me = lax.axis_index("chan")
    seg = lax.axis_index("seg")
    other_core = seg + 1 - 2 * (seg % 2)
    other_chip = (seg + 2) % 4
    tiles = chans * R

    def load(i):
        at = pl.ds(*STEPS[i])
        return [
            pltpu.make_async_copy(
                traces.at[at, :, pl.ds(q * QUARTER, QUARTER)], x_ref.at[at, q], x_sem.at[i, q]
            )
            for q in range(4)
        ]

    def load_fine():
        return (
            pltpu.make_async_copy(inv_fine.at[:, :, seg], fine_ref, fine_sem.at[0]),
            pltpu.make_async_copy(inv_coarse_hbm, inv_coarse, fine_sem.at[1]),
        )

    for copy in load(0):
        copy.start()

    barrier = pltpu.get_barrier_semaphore()

    def greet(r):
        pl.semaphore_signal(barrier, inc=1, device_id={"chan": peer(me, r)}, device_id_type=MESH)


    def hops(n):
        return min(n % 4, 4 - n % 4) + min(n // 4 % 4, 4 - n // 4 % 4) + n // 16

    for distance in sorted(range(1, chans), key=hops, reverse=True):
        greet(distance)
    for to in (other_core, other_chip):
        pl.semaphore_signal(barrier, inc=1, device_id={"seg": to}, device_id_type=MESH)

    info_ref[:, pl.ds(0, CB)] = mask_row[...]
    info_ref[:, pl.ds(CB, CB)] = jnp.zeros((1, CB), jnp.int32)
    info_ref[:, pl.ds(CB, R * G)] = owners[...] * BIN_DEV + locals_[...]

    def make_rows(a, half):
        at = pl.ds(a * 64 if isinstance(a, int) else pl.multiple_of(a * 64, 64), 64)
        for chunk in range(4 * half, 4 * half + 4):
            cols = pl.ds(chunk * 128, 128)
            ar, ai = coarse_re[a, :, cols], coarse_im[a, :, cols]
            br, bi = fine_re[:, cols], fine_im[:, cols]
            base = (chunk % 4) * 128
            tab[2 * half][at, pl.ds(base, 128)] = (ar * br - ai * bi).astype(jnp.bfloat16)
            tab[2 * half + 1][at, pl.ds(base, 128)] = (ar * bi + ai * br).astype(jnp.bfloat16)

    loop(0, QUARTER // 64, lambda a: make_rows(a, 0))

    turn = lax.broadcasted_iota(jnp.int32, (16, 256), 1) % 4
    c0 = jnp.where(turn == 0, 1.0, jnp.where(turn == 2, -1.0, 0.0))
    c1 = jnp.where(turn == 1, 1.0, jnp.where(turn == 3, -1.0, 0.0))
    flip = jnp.where(turn % 2 == 0, 1.0, -1.0)

    own = jnp.broadcast_to(info_ref[:, pl.ds(0, CB)].astype(jnp.float32), (CB, CB))
    diagonal = lax.broadcasted_iota(jnp.int32, (CB, CB), 0) == lax.broadcasted_iota(
        jnp.int32, (CB, CB), 1
    )
    column = jnp.sum(jnp.where(diagonal, own, 0.0), axis=1, keepdims=True)
    valid_ref[...] = jnp.broadcast_to(column, (CB, CB))

    power[:, pl.ds(0, 128)] = jnp.zeros((2 * CB, 128), jnp.bfloat16)
    power[:, pl.ds(128 + NB, 128)] = jnp.zeros((2 * CB, 128), jnp.bfloat16)
    near = (
        lax.broadcasted_iota(jnp.int32, (512, 256), 0)
        - lax.broadcasted_iota(jnp.int32, (512, 256), 1)
        - 128
    )
    band = jnp.where(jnp.abs(near) <= HW, 1.0, 0.0).astype(jnp.bfloat16)

    send = [send_one.at[0], send_one.at[1], send_two.at[0], send_two.at[1], send_one.at[2], send_one.at[3]]
    recv = [recv_one.at[0], recv_one.at[1], recv_two.at[0], recv_two.at[1], recv_one.at[2], recv_one.at[3]]

    def exchange(i, r):
        to = peer(me, r)
        return pltpu.make_async_remote_copy(
            send[i].at[to],
            recv[i].at[me],
            send_sem.at[i],
            recv_sem.at[i],
            device_id={"chan": to},
            device_id_type=MESH,
        )

    def keep(i):
        return pltpu.make_async_copy(send[i].at[me], recv[i].at[me], own_sem.at[i])

    def await_all(ref, sem):
        pieces = ref.at[pl.ds(0, chans - 1)]
        pltpu.make_async_copy(pieces, pieces, sem).wait()

    def tell(r):
        to = peer(me, r)
        return pltpu.make_async_remote_copy(
            info_ref,
            info.at[me],
            info_send,
            info_recv,
            device_id={"chan": to},
            device_id_type=MESH,
        )

    def await_step(ref, i, sem):
        pieces = ref[i].at[pl.ds(0, chans - 1)]
        pltpu.make_async_copy(pieces, pieces, sem.at[i]).wait()

    def whiten_step(i):
        first, segs = STEPS[i]
        rows = segs * CB
        every = pl.ds(0, rows)
        for copy in load(i):
            copy.wait()
        if i == 0:
            for copy in [copy for j in range(1, len(STEPS)) for copy in load(j)]:
                copy.start()
            for copy in load_fine():
                copy.start()

        def transform(n):
            block = x_ref[pl.ds(first, segs)].reshape(4 * rows, QUARTER)
            parts[pl.ds(0, 4 * rows), pl.ds(n * 512, 512)] = jnp.dot(
                block, tab[n][...], preferred_element_type=jnp.float32
            )

        for n in range(4):
            transform(n)
            if i == 0 and n < 2:
                for a in range(8 * n, 8 * n + 8):
                    make_rows(a, 1)

        def add_power(n):
            at = pl.ds(pl.multiple_of(n * 16, 16), 16)
            s, row = n // (CB // 16), n % (CB // 16)
            for chunk in range(NB // 256):
                base = (chunk // 2) * NB + (chunk % 2) * 256
                res, ims = [], []
                for q in range(4):
                    rows_of = pl.ds(pl.multiple_of((s * 4 + q) * CB + row * 16, 16), 16)
                    res.append(parts[rows_of, pl.ds(base, 256)])
                    ims.append(parts[rows_of, pl.ds(base + HALF, 256)])
                b_re, b_im = res[1] + flip * res[3], ims[1] + flip * ims[3]
                re = res[0] + flip * res[2] + (c0 * b_re + c1 * b_im)
                im = ims[0] + flip * ims[2] + (c0 * b_im - c1 * b_re)
                spec[at, pl.ds(base, 256)] = re
                spec[at, pl.ds(base + HALF, 256)] = im
                power[at, pl.ds(128 + chunk * 256, 256)] = (re * re + im * im).astype(jnp.bfloat16)

        loop(0, rows // 16, add_power)

        for chunk in range(NB // 256):
            total = jnp.dot(
                power[every, pl.ds(chunk * 256, 512)], band, preferred_element_type=jnp.float32
            )
            k = chunk * 256 + lax.broadcasted_iota(jnp.int32, (1, 256), 1)
            count = jnp.minimum(k + HW, NB - 1) - jnp.maximum(k - HW, 0) + 1
            inv_level[every, pl.ds(chunk * 256, 256)] = lax.rsqrt(
                total * (1.0 / count.astype(jnp.float32)) + EPSILON
            )

        def scale(g):
            valid = valid_ref[pl.ds(pl.multiple_of(g * 8, 8), 8), :]
            for s in range(segs):
                row = pl.ds(pl.multiple_of(s * CB + g * 8, 8), 8)
                for chunk in range(NB // 128):
                    h, at = chunk // 4, (chunk % 4) * 128
                    weight = inv_level[row, pl.ds(chunk * 128, 128)] * valid
                    re = spec[row, pl.ds(h * NB + at, 128)] * weight
                    im = spec[row, pl.ds(h * NB + HALF + at, 128)] * weight
                    to = 2 * g + h
                    block = send[i].at[to, s] if segs == 2 else send[i].at[to]
                    block[:, pl.ds(at, 128)] = re.astype(jnp.bfloat16)
                    block[:, pl.ds(HALF + at, 128)] = im.astype(jnp.bfloat16)

        loop(0, G, scale)
        keep(i).start()

    def send_step(i):
        loop(1, chans, lambda r: exchange(i, chans - r).start())

    whiten_step(0)
    pl.semaphore_wait(barrier, chans + 1)
    pl.semaphore_signal(entered, inc=1, device_id={"seg": other_chip}, device_id_type=MESH)
    send_step(0)
    for i in range(1, len(STEPS)):
        whiten_step(i)
        send_step(i)
        if i == 2:
            loop(1, chans, lambda r: tell(r).start())

    for block in recv:
        block[pl.ds(chans, R)] = jnp.zeros((R,) + block.shape[1:], jnp.bfloat16)
    for copy in load_fine():
        copy.wait()

    def make_inverse(n):
        h, at = n // 8, pl.multiple_of((n % 8) * 16, 16)
        br, bi = fine_ref[0, h, pl.ds(at, 16)], fine_ref[1, h, pl.ds(at, 16)]
        for a in range(16):
            ar, ai = inv_coarse[0, a], inv_coarse[1, a]
            re, im = ar * br - ai * bi, -(ar * bi + ai * br)
            for which, value in enumerate((re, im)):
                at_row = pl.ds(pl.multiple_of(h * 256 + which * 128 + at, 16), 16)
                high = value.astype(jnp.bfloat16)
                inv_hi[at_row, pl.ds(a * 128, 128)] = high
                low = value - high.astype(jnp.float32)
                inv_lo[at_row, pl.ds(a * 128, 128)] = low.astype(jnp.bfloat16)

    loop(0, 16, make_inverse)

    def products(steps, chunk, first, add=True):
        re_at = pl.ds(pl.multiple_of(chunk * 128, 128), 128)
        im_at = pl.ds(pl.multiple_of(HALF + chunk * 128, 128), 128)
        blocks = []
        for i in steps:
            two = STEPS[i][1] == 2
            for s in range(STEPS[i][1]):
                blocks.append(
                    [recv[i].at[first + j, s] if two else recv[i].at[first + j] for j in range(4 + R)]
                )
        re = [[ref[:, re_at].astype(jnp.float32) for ref in refs] for refs in blocks]
        im = [[ref[:, im_at].astype(jnp.float32) for ref in refs] for refs in blocks]
        for j in range(4):
            for d in range(1, R + 1):
                t = (d - 1) * chans + first + j
                p, q = (0.0, 0.0) if not add else (
                    acc[chunk, t, :, pl.ds(0, 128)], acc[chunk, t, :, pl.ds(128, 128)]
                )
                for s in range(len(blocks)):
                    p = p + (re[s][j] * re[s][j + d] + im[s][j] * im[s][j + d])
                    q = q + (im[s][j] * re[s][j + d] - re[s][j] * im[s][j + d])
                acc[chunk, t, :, pl.ds(0, 128)] = p
                acc[chunk, t, :, pl.ds(128, 128)] = q

    def here(i):
        await_step(recv, i, recv_sem)
        keep(i).wait()

    here(0)
    here(1)
    loop(0, chans, lambda n: products((0, 1), n % 4, (n // 4) * 4, add=False))
    for i in (2, 3, 4):
        here(i)
        loop(0, chans, lambda n: products((i,), n % 4, (n // 4) * 4))

    info[pl.ds(me, 1)] = info_ref[...].reshape(1, 1, 256)
    info[pl.ds(chans, 8)] = jnp.zeros((8, 1, 256), jnp.int32)
    await_all(info, info_recv)
    group = me // 2
    lanes = lax.broadcasted_iota(jnp.int32, (chans, CB), 1)
    everyone = info[...].reshape(chans + 8, 256).astype(jnp.float32)
    masks, names = everyone[:, :CB], everyone[:chans, CB:]
    picked = []
    for d in range(1, R + 1):
        both = masks[:chans] * masks[d : d + chans]
        count = jnp.sum(jnp.where(lanes // 8 == group, both, 0.0), axis=1, keepdims=True)
        factor = 1.0 / (total_segs * jnp.maximum(count, 1.0))
        scale_ref[pl.ds((d - 1) * chans, chans), :] = jnp.broadcast_to(factor, (chans, 256))
        mine = lanes == (d - 1) * G + group
        name = jnp.sum(jnp.where(mine, names, 0.0), axis=1, keepdims=True)
        bin_of = lax.broadcasted_iota(jnp.int32, (chans, 256), 1).astype(jnp.float32)
        picked.append(jnp.where(jnp.broadcast_to(name, (chans, 256)) == bin_of, 1.0, 0.0))
    onehot[...] = jnp.concatenate(picked, 0).T.astype(jnp.bfloat16)

    here(len(STEPS) - 1)

    def hand_over(n, chunk):
        return pltpu.make_async_remote_copy(
            raw.at[chunk],
            raw_in.at[n],
            raw_send.at[n],
            raw_recv.at[n],
            device_id={"seg": other_core},
            device_id_type=MESH,
        )

    def finish_quarter(chunk):
        loop(0, chans // 4, lambda n: products((len(STEPS) - 1,), chunk, n * 4))

        def reduce_rows(n):
            at = pl.ds(pl.multiple_of(n * 8, 8), 8)
            raw[chunk, at, :] = acc[chunk, at].sum(1)

        loop(0, tiles // 8, reduce_rows)

    chip = seg - seg % 2
    far = 2 - chip

    def give(n, chunk):
        finish_quarter(chunk)
        hand_over(n, chunk).start()

    def stack(n, sums):
        sums = sums * scale_ref[...]
        high = sums.astype(jnp.bfloat16)
        low = (sums - high.astype(jnp.float32)).astype(jnp.bfloat16)
        stacked = jnp.dot(onehot[...], high, preferred_element_type=jnp.float32)
        stacked += jnp.dot(onehot[...], low, preferred_element_type=jnp.float32)
        bins[n] = stacked.reshape(chans, BIN_DEV, 256).astype(jnp.bfloat16)

    def deliver(n, r):
        to = peer(me, r)
        return pltpu.make_async_remote_copy(
            bins.at[n, to],
            bins_in.at[n * chans + me],
            bins_send,
            bins_recv,
            device_id={"seg": other_chip if n else seg, "chan": to},
            device_id_type=MESH,
        )

    give(0, far + other_core % 2)
    finish_quarter(other_chip)
    give(1, other_core)
    hand_over(0, far + other_core % 2).wait()
    stack(1, raw[other_chip] + raw_in[0])
    pl.semaphore_wait(entered, 1)
    loop(0, chans, lambda r: deliver(1, chans - 1 - r).start())
    finish_quarter(seg)
    hand_over(1, other_core).wait()
    stack(0, raw[seg] + raw_in[1])
    loop(1, chans, lambda r: deliver(0, chans - r).start())
    bins_in[me] = bins[0, me]
    pieces = bins_in.at[pl.ds(0, 2 * chans - 1)]
    pltpu.make_async_copy(pieces, pieces, bins_recv).wait()
    halves = []
    for h in range(2):
        total = bins_in[h].astype(jnp.float32)
        for g in range(1, 2 * G):
            total = total + bins_in[2 * g + h].astype(jnp.float32)
        halves.append(total)
    spectra = jnp.concatenate(halves, axis=1)
    high = spectra.astype(jnp.bfloat16)
    low = (spectra - high.astype(jnp.float32)).astype(jnp.bfloat16)
    both = jnp.concatenate([high, low], axis=0)

    def share(n, q):
        return pltpu.make_async_remote_copy(
            part.at[n],
            part_in.at[n, seg],
            part_send.at[n, q],
            part_recv.at[n, seg],
            device_id={"seg": (seg + q) % 4},
            device_id_type=MESH,
        )

    width = NLAG // 2
    for n in range(2):
        at = pl.ds(n * width, width)
        value = jnp.dot(both, inv_hi[:, at], preferred_element_type=jnp.float32)
        value = value[:BIN_DEV] + value[BIN_DEV:]
        value += jnp.dot(high, inv_lo[:, at], preferred_element_type=jnp.float32)
        part[n] = value.astype(jnp.bfloat16)
        for q in (2, 1, 3):
            share(n, q).start()
        part_in[n, seg] = value.astype(jnp.bfloat16)
    for n in range(2):
        for q in (1, 2, 3):
            source = part_in.at[n, (seg + q) % 4]
            pltpu.make_async_copy(source, source, part_recv.at[n, (seg + q) % 4]).wait()
        terms = [part_in[n, q].astype(jnp.float32) for q in range(4)]
        out_ref[:, pl.ds(n * width, width)] = (terms[0] + terms[1]) + (terms[2] + terms[3])

    for n in range(2):
        for q in (1, 2, 3):
            share(n, q).wait_send()
    for i in range(len(STEPS)):
        await_step(send, i, send_sem)
    await_all(info, info_send)
    pltpu.make_async_copy(pieces, pieces, bins_send).wait()


def per_device(traces, channel_mask, owner_ids, local_bins):
    chans, quarters = lax.axis_size("chan"), lax.axis_size("seg")
    tiles, steps = chans * R, len(STEPS)
    vmem = pl.BlockSpec(memory_space=pltpu.VMEM)
    anywhere = pl.BlockSpec(memory_space=pl.ANY)
    dma = pltpu.SemaphoreType.DMA
    bf16, f32 = jnp.bfloat16, jnp.float32
    return pl.pallas_call(
        functools.partial(stack_kernel, float(traces.shape[0] * quarters)),
        out_shape=jax.ShapeDtypeStruct((BIN_DEV, NLAG), f32),
        in_specs=[anywhere] + [vmem] * 4 + [anywhere] * 2 + [vmem] * 3,
        out_specs=vmem,
        scratch_shapes=[
            pltpu.VMEM((traces.shape[0], 4, CB, QUARTER), bf16),
            *[pltpu.VMEM((QUARTER, 512), bf16)] * 4,
            pltpu.VMEM((8 * CB, 2 * NB), f32),
            pltpu.VMEM((2 * CB, 2 * NB), f32),
            pltpu.VMEM((2 * CB, NB + 256), bf16),
            pltpu.VMEM((2 * CB, NB), f32),
            pltpu.VMEM((CB, CB), f32),
            pltpu.VMEM((4, chans, 8, NB), bf16),
            pltpu.VMEM((4, chans + R, 8, NB), bf16),
            pltpu.VMEM((2, chans, 2, 8, NB), bf16),
            pltpu.VMEM((2, chans + R, 2, 8, NB), bf16),
            pltpu.VMEM((4, tiles, 8, 256), f32),
            pltpu.VMEM((1, 2 * CB), jnp.int32),
            pltpu.VMEM((2, 2, 128, 128), f32),
            pltpu.VMEM((2, 16, 16, 128), f32),
            pltpu.VMEM((512, NLAG), bf16),
            pltpu.VMEM((512, NLAG), bf16),
            pltpu.VMEM((chans + 8, 1, 256), jnp.int32),
            pltpu.VMEM((256, tiles), bf16),
            pltpu.VMEM((tiles, 256), f32),
            pltpu.VMEM((4, tiles, 256), f32),
            pltpu.VMEM((2, tiles, 256), f32),
            pltpu.VMEM((2, chans, BIN_DEV, 256), bf16),
            pltpu.VMEM((2 * chans, BIN_DEV, 256), bf16),
            pltpu.VMEM((2, BIN_DEV, NLAG // 2), bf16),
            pltpu.VMEM((2, 4, BIN_DEV, NLAG // 2), bf16),
            dma((steps, 4)), dma((2,)), dma((steps,)), dma((steps,)), dma((steps,)),
            dma, dma, dma((2,)), dma((2,)), dma, dma, dma((2, 4)), dma((2, 4)),
            pltpu.SemaphoreType.REGULAR,
        ],
        compiler_params=pltpu.CompilerParams(
            collective_id=0, has_side_effects=True, vmem_limit_bytes=60 << 20
        ),
        name="stack",
    )(
        traces,
        *forward_factors(),
        *inverse_factors(),
        channel_mask.reshape(1, -1),
        owner_ids.reshape(1, -1),
        local_bins,
    )


def solution(mesh):
    in_specs = (P("seg", "chan", None), P("chan"), P("chan", None, None), P("chan", None))
    return jax.shard_map(
        per_device, mesh=mesh, in_specs=in_specs, out_specs=P("chan", None), check_vma=False
    )
```
